512 devices in a mesh: dp: 8 (over z_hi, y), mp: 64 (over z_lo, x, core).
Axes of the slice: x: 4, y: 4, z: 16 (z_hi: 2, z_lo: 8; z = z_hi * 8 + z_lo), core: 2. Of those that a mesh axis runs over, the one named last changes fastest.
Arguments:
- tokens: bfloat16 [512, 6144], P(('dp', 'mp')), may hold values from -6 to 6
- w_in: bfloat16 [6144, 24576], P('dp', 'mp'), may hold values from -0.078125 to 0.078125
- w_out: bfloat16 [24576, 6144], P('mp', 'dp'), may hold values from -0.0390625 to 0.0390625
- cotangent: bfloat16 [512, 6144], P(('dp', 'mp')), may hold values from -6 to 6
Outputs:
- mixed: bfloat16 [512, 6144], P(('dp', 'mp'))
- grad_tokens: bfloat16 [512, 6144], P(('dp', 'mp'))
- grad_w_in: float32 [6144, 24576], P('dp', 'mp')
- grad_w_out: float32 [24576, 6144], P('mp', 'dp')
The draws below stay inside these ranges and needn't reach their ends.
All inputs are finite; a program needn't handle non-finite values.
Results may differ from the reference program's by a relative error of at most 0.0054.
Values may be sent and summed in bfloat16 or wider, within the bound.
No kernel may reach another device: no remote copies, remote signals or barrier semaphores. Data moves between devices by JAX's collectives and lax.ppermute only.
A program may use at most 64 MiB of HBM per device.

```python
import jax
import jax.numpy as jnp
from jax import lax

D = 6144
FF = 24576
TOKENS = 512


def shard_levels(stream_key, shape, shards, low, high):
    level = 1.0
    for axis_at, parts in shards:
        draws = jax.random.uniform(jax.random.fold_in(jax.random.fold_in(stream_key, 6), axis_at), (parts,), jnp.float32, low / len(shards), high / len(shards))
        level = level * jnp.repeat(jnp.exp(draws), shape[axis_at] // parts).reshape((-1,) + (1,) * (len(shape) - 1 - axis_at))
    return level


def normal_values(stream_key, extent, spread, reach, shards=(), held_as=jnp.bfloat16):
    result = jax.random.normal(stream_key, extent, jnp.float32) * spread
    if len(shards) > 0:
        result = shard_levels(stream_key, extent, shards, -0.22, 0.18) * result
    return jnp.clip(result, min=-reach, max=reach).astype(held_as)


def setup_inputs(seed: int = 0) -> dict:
    seeds = jax.random.split(jax.random.key(seed), 5)
    return {
        "tokens": normal_values(seeds[0], (TOKENS, D), 1.0, 6.0, ((0, 512),)),
        "w_in": normal_values(seeds[1], (D, FF), D ** -0.5, 0.078125, ((0, 8), (1, 64))),
        "w_out": normal_values(seeds[2], (FF, D), FF ** -0.5, 0.0390625, ((0, 64), (1, 8))),
        "cotangent": normal_values(seeds[3], (TOKENS, D), 1.0, 6.0, ((0, 512),)),
    }


epsilon = 1e-06

def gelu_tanh(values):
    return jax.nn.gelu(values, approximate=True)

def gelu_grad(pre_values, upstream):
    return jax.vjp(gelu_tanh, pre_values)[1](upstream)[0]

def reference(tokens, w_in, w_out, cotangent):
    tokens_wide = tokens.astype(jnp.float32)
    row_mean = lax.optimization_barrier(jnp.mean(tokens_wide, axis=1, keepdims=True))
    centered = tokens_wide - row_mean
    inv_scale = lax.rsqrt(lax.optimization_barrier(jnp.mean(centered * centered, axis=1, keepdims=True)) + epsilon)
    unit_rows = centered * inv_scale
    normed = unit_rows.astype(jnp.bfloat16)
    pre_values = jnp.dot(normed, w_in, preferred_element_type=jnp.float32)
    act_values = gelu_tanh(pre_values).astype(jnp.bfloat16)
    branch_out = jnp.dot(act_values, w_out, preferred_element_type=jnp.float32)
    mixed = (tokens_wide + branch_out).astype(jnp.bfloat16)
    act_grad = jnp.dot(cotangent, w_out.T, preferred_element_type=jnp.float32)
    pre_grad = gelu_grad(pre_values, act_grad).astype(jnp.bfloat16)
    grad_w_out = jnp.dot(act_values.T, cotangent, preferred_element_type=jnp.float32)
    grad_w_in = jnp.dot(normed.T, pre_grad, preferred_element_type=jnp.float32)
    normed_grad = jnp.dot(pre_grad, w_in.T, preferred_element_type=jnp.float32)
    row_inner = lax.optimization_barrier(jnp.mean(normed_grad * unit_rows, axis=1, keepdims=True))
    through = inv_scale * (normed_grad - lax.optimization_barrier(jnp.mean(normed_grad, axis=1, keepdims=True)) - unit_rows * row_inner)
    grad_tokens = (cotangent.astype(jnp.float32) + through).astype(jnp.bfloat16)
    return (mixed, grad_tokens, grad_w_in, grad_w_out)
```

```python
import jax
import jax.numpy as jnp
from jax import lax
from jax.sharding import Mesh, PartitionSpec as P

epsilon = 1e-06
AXES = ("zh", "y", "zl", "x", "core")
SIZES = (2, 4, 8, 4, 2)
ZH, Y, ZL, X, CORE = SIZES
f32 = jnp.float32
bf16 = jnp.bfloat16


def gelu_tanh(values):
    return jax.nn.gelu(values, approximate=True)


def gelu_grad(pre_values, upstream):
    return jax.vjp(gelu_tanh, pre_values)[1](upstream)[0]


def swap(values, axis):
    return lax.ppermute(values, axis, [(0, 1), (1, 0)])


def trade(values, axis):
    return lax.all_to_all(values, axis, split_axis=0, concat_axis=0, tiled=True)


def gather(values, axis, count):
    return trade(jnp.broadcast_to(values[None], (count,) + values.shape), axis)


def total(parts):
    return jnp.sum(parts.astype(f32), axis=0)


def local(tokens, w_in, w_out, cotangent):
    contract_last = (((1,), (1,)), ((), ()))
    contract_first = (((0,), (0,)), ((), ()))
    width = w_in.shape[0]
    hidden = w_in.shape[1]
    groups = ZH * Y

    tokens_wide = tokens.astype(f32)
    row_mean = jnp.mean(tokens_wide, axis=1, keepdims=True)
    centered = tokens_wide - row_mean
    inv_scale = lax.rsqrt(jnp.mean(centered * centered, axis=1, keepdims=True) + epsilon)
    unit_rows = centered * inv_scale
    normed = unit_rows.astype(bf16)

    both = jnp.concatenate([normed.reshape(groups, 1, width), cotangent.reshape(groups, 1, width)], axis=1)
    both = trade(both, ("zh", "y")).transpose(1, 0, 2)
    both = gather(both, "zl", ZL).transpose(1, 0, 2, 3).reshape(2, ZL * groups, width)
    both = gather(both, "x", X).transpose(1, 0, 2, 3).reshape(2, X * ZL * groups, width)
    other = swap(both, "core")
    rows = jnp.concatenate([both, other], axis=1)
    flat_normed, flat_grad = rows[0], rows[1]
    count = flat_normed.shape[0]

    pre_part = jnp.dot(flat_normed, w_in, preferred_element_type=f32)
    grad_part = lax.dot_general(flat_grad, w_out, contract_last, preferred_element_type=f32)

    parts = jnp.stack([pre_part.astype(bf16), grad_part.astype(bf16)]).reshape(2, Y, count // Y, hidden)
    parts = total(trade(parts.transpose(1, 0, 2, 3), "y"))
    parts = parts.reshape(2, ZH, count // groups, hidden)
    mine = lax.axis_index("zh")
    keep = lax.dynamic_index_in_dim(parts, mine, 1, keepdims=False)
    give = lax.dynamic_index_in_dim(parts, 1 - mine, 1, keepdims=False).astype(bf16)
    summed = keep + swap(give, "zh").astype(f32)
    pre, act_grad = summed[0], summed[1]
    act = gelu_tanh(pre).astype(bf16)
    pre_grad = gelu_grad(pre, act_grad).astype(bf16)

    own = jnp.stack([act, pre_grad])
    far = swap(own, "zh")
    first = mine == 0
    pair = jnp.stack([jnp.where(first, own, far), jnp.where(first, far, own)], axis=1)
    pair = pair.reshape(2, count // Y, hidden)
    full = gather(pair, "y", Y).transpose(1, 0, 2, 3).reshape(2, count, hidden)
    act_all, pre_grad_all = full[0], full[1]

    out_part = jnp.dot(act_all, w_out, preferred_element_type=f32)
    back_part = lax.dot_general(pre_grad_all, w_in, contract_last, preferred_element_type=f32)
    half = count // CORE
    give = jnp.stack([out_part[half:].astype(bf16), back_part[half:].astype(bf16)])
    sums = jnp.stack([out_part[:half], back_part[:half]]) + swap(give, "core").astype(f32)
    sums = sums.astype(bf16).reshape(2, X, half // X, width).transpose(1, 0, 2, 3)
    sums = total(trade(sums, "x"))
    sums = sums.astype(bf16).reshape(2, ZL, groups, width).transpose(1, 0, 2, 3)
    sums = total(trade(sums, "zl"))
    whole = trade(sums.transpose(1, 0, 2), ("zh", "y")).transpose(1, 0, 2).reshape(2, 1, groups * width)

    grad_w_out = lax.dot_general(act_all, flat_grad, contract_first, preferred_element_type=f32)
    grad_w_in = lax.dot_general(flat_normed, pre_grad_all, contract_first, preferred_element_type=f32)

    mixed = (tokens_wide + whole[0]).astype(bf16)
    normed_grad = whole[1]
    row_inner = jnp.mean(normed_grad * unit_rows, axis=1, keepdims=True)
    through = inv_scale * (
        normed_grad - jnp.mean(normed_grad, axis=1, keepdims=True) - unit_rows * row_inner
    )
    grad_tokens = (cotangent.astype(f32) + through).astype(bf16)
    return (mixed, grad_tokens, grad_w_in, grad_w_out)


def solution(mesh):
    fine = Mesh(mesh.devices.reshape(SIZES), AXES)
    dp, mp = ("zh", "y"), ("zl", "x", "core")
    return jax.shard_map(
        local,
        mesh=fine,
        in_specs=(P(dp + mp, None), P(dp, mp), P(mp, dp), P(dp + mp, None)),
        out_specs=(P(dp + mp, None), P(dp + mp, None), P(dp, mp), P(mp, dp)),
        check_vma=False,
    )
```

```python
import jax
import jax.numpy as jnp
from jax import lax
from jax.sharding import Mesh, PartitionSpec as P

epsilon = 1e-06
AXES = ("zh", "y", "zl", "x", "core")
SIZES = (2, 4, 8, 4, 2)
ZH, Y, ZL, X, CORE = SIZES
FAR = ("zh", "y", "zl")
f32 = jnp.float32
bf16 = jnp.bfloat16


def gelu_tanh(values):
    return jax.nn.gelu(values, approximate=True)


def gelu_grad(pre_values, upstream):
    return jax.vjp(gelu_tanh, pre_values)[1](upstream)[0]


def swap(values, axis):
    return lax.ppermute(values, axis, [(0, 1), (1, 0)])


def trade(values, axis):
    return lax.all_to_all(values, axis, split_axis=0, concat_axis=0, tiled=True)


def total(parts):
    return jnp.sum(parts.astype(f32), axis=0)


def local(tokens, w_in, w_out, cotangent):
    contract_last = (((1,), (1,)), ((), ()))
    contract_first = (((0,), (0,)), ((), ()))
    width = w_in.shape[0]
    hidden = w_in.shape[1]
    groups = ZH * Y

    tokens_wide = tokens.astype(f32)
    row_mean = jnp.mean(tokens_wide, axis=1, keepdims=True)
    centered = tokens_wide - row_mean
    inv_scale = lax.rsqrt(jnp.mean(centered * centered, axis=1, keepdims=True) + epsilon)
    unit_rows = centered * inv_scale
    normed = unit_rows.astype(bf16)

    both = jnp.concatenate([normed.reshape(1, groups, 1, width), cotangent.reshape(1, groups, 1, width)])
    both = jnp.broadcast_to(both, (2, groups, ZL, width)).reshape(2, groups * ZL, width)
    both = lax.all_to_all(both, FAR, split_axis=1, concat_axis=1, tiled=True)
    both = lax.all_gather(both, "x", axis=1, tiled=True)
    other = swap(both, "core")
    rows = jnp.concatenate([both, other], axis=1)
    flat_normed, flat_grad = rows[0], rows[1]
    count = flat_normed.shape[0]

    pre_part = jnp.dot(flat_normed, w_in, preferred_element_type=f32)
    grad_part = lax.dot_general(flat_grad, w_out, contract_last, preferred_element_type=f32)

    parts = jnp.stack([pre_part.astype(bf16), grad_part.astype(bf16)]).reshape(2, Y, count // Y, hidden)
    parts = total(trade(parts.transpose(1, 0, 2, 3), "y"))
    summed = parts + swap(parts.astype(bf16), "zh").astype(f32)
    pre, act_grad = summed[0], summed[1]
    act = gelu_tanh(pre).astype(bf16)
    pre_grad = gelu_grad(pre, act_grad).astype(bf16)

    full = lax.all_gather(jnp.stack([act, pre_grad]), "y", axis=1, tiled=True)
    act_all, pre_grad_all = full[0], full[1]

    out_part = jnp.dot(act_all, w_out, preferred_element_type=f32)
    back_part = lax.dot_general(pre_grad_all, w_in, contract_last, preferred_element_type=f32)
    half = count // CORE
    give = jnp.stack([out_part[half:].astype(bf16), back_part[half:].astype(bf16)])
    sums = jnp.stack([out_part[:half], back_part[:half]]) + swap(give, "core").astype(f32)
    sums = sums.astype(bf16).reshape(2, X, half // X, width).transpose(1, 0, 2, 3)
    sums = total(trade(sums, "x"))
    sums = lax.all_to_all(sums.astype(bf16), FAR, split_axis=1, concat_axis=1, tiled=True)
    whole = jnp.sum(sums.astype(f32).reshape(2, groups, ZL, width), axis=2).reshape(2, 1, groups * width)

    grad_w_out = lax.dot_general(act_all, flat_grad, contract_first, preferred_element_type=f32)
    grad_w_in = lax.dot_general(flat_normed, pre_grad_all, contract_first, preferred_element_type=f32)

    mixed = (tokens_wide + whole[0]).astype(bf16)
    normed_grad = whole[1]
    row_inner = jnp.mean(normed_grad * unit_rows, axis=1, keepdims=True)
    through = inv_scale * (
        normed_grad - jnp.mean(normed_grad, axis=1, keepdims=True) - unit_rows * row_inner
    )
    grad_tokens = (cotangent.astype(f32) + through).astype(bf16)
    return (mixed, grad_tokens, grad_w_in, grad_w_out)


def solution(mesh):
    fine = Mesh(mesh.devices.reshape(SIZES), AXES)
    dp, mp = ("zh", "y"), ("zl", "x", "core")
    return jax.shard_map(
        local,
        mesh=fine,
        in_specs=(P(dp + mp, None), P(dp, mp), P(mp, dp), P(dp + mp, None)),
        out_specs=(P(dp + mp, None), P(dp + mp, None), P(dp, mp), P(mp, dp)),
        check_vma=False,
    )
```

```python
import jax
import jax.numpy as jnp
from jax import lax
from jax.sharding import Mesh, PartitionSpec as P

epsilon = 1e-06
AXES = ("zh", "y", "zl", "x", "core")
SIZES = (2, 4, 8, 4, 2)
ZH, Y, ZL, X, CORE = SIZES
FAR = ("zh", "zl")
f32 = jnp.float32
bf16 = jnp.bfloat16


def gelu_tanh(values):
    return jax.nn.gelu(values, approximate=True)


def gelu_grad(pre_values, upstream):
    return jax.vjp(gelu_tanh, pre_values)[1](upstream)[0]


def swap(values, axis):
    return lax.ppermute(values, axis, [(0, 1), (1, 0)])


def shift(values, axis, step):
    count = lax.axis_size(axis)
    return lax.ppermute(values, axis, [(at, (at + step) % count) for at in range(count)])


def trade(values, axis):
    return lax.all_to_all(values, axis, split_axis=0, concat_axis=0, tiled=True)


def total(parts):
    return jnp.sum(parts.astype(f32), axis=0)


def local(tokens, w_in, w_out, cotangent):
    contract_last = (((1,), (1,)), ((), ()))
    contract_first = (((0,), (0,)), ((), ()))
    width = w_in.shape[0]
    hidden = w_in.shape[1]
    features = Y * width
    here = lax.axis_index("y")

    tokens_wide = tokens.astype(f32)
    row_mean = jnp.mean(tokens_wide, axis=1, keepdims=True)
    centered = tokens_wide - row_mean
    inv_scale = lax.rsqrt(jnp.mean(centered * centered, axis=1, keepdims=True) + epsilon)
    unit_rows = centered * inv_scale
    normed = unit_rows.astype(bf16)

    both = jnp.concatenate([normed.reshape(1, ZH, 1, features), cotangent.reshape(1, ZH, 1, features)])
    both = jnp.broadcast_to(both, (2, ZH, ZL, features)).reshape(2, ZH * ZL, features)

    block = jnp.stack([w_in, jnp.concatenate([w_out[:, :hidden], w_out[:, hidden:]], axis=0)])
    both, block = lax.optimization_barrier((both, block))
    below = shift(block, "y", 1)
    above = shift(block, "y", -1)
    far_in = shift(below[0], "y", 1)
    far_out = shift(above[1], "y", -1)
    w_ins = jnp.zeros((Y, width, hidden), bf16)
    w_outs = jnp.zeros((Y, hidden, width), bf16)
    for step, ins, outs in ((0, w_in, block[1]), (3, below[0], below[1]), (1, above[0], above[1]), (2, far_in, far_out)):
        at = lax.rem(here + step, Y)
        w_ins = lax.dynamic_update_slice(w_ins, ins[None], (at, 0, 0))
        w_outs = lax.dynamic_update_slice(w_outs, outs[None, :hidden], (at, 0, 0))
        w_outs = lax.dynamic_update_slice(w_outs, outs[None, hidden:], (at, 0, hidden))
    w_ins = w_ins.reshape(features, hidden)

    both = lax.all_to_all(both, FAR, split_axis=1, concat_axis=1, tiled=True)
    both = lax.all_gather(both, "x", axis=1, tiled=True)
    rows = jnp.concatenate([both, swap(both, "core")], axis=1)
    count = rows.shape[1]

    pre_part = jnp.dot(rows[0], w_ins, preferred_element_type=f32)
    grad_part = sum(
        lax.dot_general(rows[1, :, at : at + width], w_outs[at // width], contract_last, preferred_element_type=f32)
        for at in range(0, features, width)
    )
    parts = jnp.stack([pre_part, grad_part])
    spread = jnp.stack([rows[:, :, at : at + width] for at in range(0, features, width)])
    far, spread = lax.optimization_barrier((parts.astype(bf16), spread))
    far = swap(far, "zh")
    spread = trade(spread, "y")
    far, spread = lax.optimization_barrier((far, spread))
    summed = parts + far.astype(f32)
    pre, act_grad = summed[0], summed[1]
    act = gelu_tanh(pre).astype(bf16)
    pre_grad = gelu_grad(pre, act_grad).astype(bf16)

    out_part = jnp.concatenate([jnp.dot(act, w_outs[at], preferred_element_type=f32) for at in range(Y)], axis=1)
    back_part = lax.dot_general(pre_grad, w_ins, contract_last, preferred_element_type=f32)
    parts = jnp.stack([out_part, back_part])
    half = count // CORE
    sums = parts[:, :half] + swap(parts[:, half:].astype(bf16), "core").astype(f32)
    sums = sums.astype(bf16).reshape(2, X, half // X, features).transpose(1, 0, 2, 3)
    sums = total(trade(sums, "x"))
    sums, pair = lax.optimization_barrier((sums.astype(bf16), jnp.stack([act, pre_grad])))
    sums = lax.all_to_all(sums, FAR, split_axis=1, concat_axis=1, tiled=True)
    whole = jnp.sum(sums.astype(f32).reshape(2, ZH, ZL, features), axis=2).reshape(2, 1, ZH * features)

    flat_normed = spread[:, 0].reshape(Y * count, width)
    flat_grad = spread[:, 1].reshape(Y * count, width)
    full = lax.all_gather(pair, "y", axis=1, tiled=True)
    grad_w_out = lax.dot_general(full[0], flat_grad, contract_first, preferred_element_type=f32)
    grad_w_in = lax.dot_general(flat_normed, full[1], contract_first, preferred_element_type=f32)

    mixed = (tokens_wide + whole[0]).astype(bf16)
    normed_grad = whole[1]
    row_inner = jnp.mean(normed_grad * unit_rows, axis=1, keepdims=True)
    through = inv_scale * (
        normed_grad - jnp.mean(normed_grad, axis=1, keepdims=True) - unit_rows * row_inner
    )
    grad_tokens = (cotangent.astype(f32) + through).astype(bf16)
    return (mixed, grad_tokens, grad_w_in, grad_w_out)


def solution(mesh):
    fine = Mesh(mesh.devices.reshape(SIZES), AXES)
    dp, mp = ("zh", "y"), ("zl", "x", "core")
    return jax.shard_map(
        local,
        mesh=fine,
        in_specs=(P(dp + mp, None), P(dp, mp), P(mp, dp), P(dp + mp, None)),
        out_specs=(P(dp + mp, None), P(dp + mp, None), P(dp, mp), P(mp, dp)),
        check_vma=False,
    )
```

```python
import jax
import jax.numpy as jnp
from jax import lax
from jax.experimental import pallas as pl
from jax.experimental.pallas import tpu as pltpu
from jax.sharding import Mesh, PartitionSpec as P

epsilon = 1e-06
AXES = ("zh", "y", "zl", "x", "core")
SIZES = (2, 4, 8, 4, 2)
ZH, Y, ZL, X, CORE = SIZES
FAR = ("zh", "zl")
f32 = jnp.float32
bf16 = jnp.bfloat16
LAST = (((1,), (1,)), ((), ()))
FIRST = (((0,), (0,)), ((), ()))
RATE = 0.7978845608028654
CUBE = 0.044715


def swap(values, axis):
    return lax.ppermute(values, axis, [(0, 1), (1, 0)])


def shift(values, axis, step):
    count = lax.axis_size(axis)
    return lax.ppermute(values, axis, [(at, (at + step) % count) for at in range(count)])


def trade(values, axis):
    return lax.all_to_all(values, axis, split_axis=0, concat_axis=0, tiled=True)


def total(parts):
    return jnp.sum(parts.astype(f32), axis=0)


def dot(left, right, contract=(((1,), (0,)), ((), ()))):
    return lax.dot_general(left, right, contract, preferred_element_type=f32)


def call(body, shapes, *args, flops=0):
    moved = sum(a.size * a.dtype.itemsize for a in args) + sum(s.size * s.dtype.itemsize for s in shapes)
    specs = [
        pl.BlockSpec(memory_space=pltpu.SMEM if a.dtype == jnp.int32 else pltpu.VMEM) for a in args
    ]
    return pl.pallas_call(
        body,
        out_shape=shapes,
        in_specs=specs,
        out_specs=[pl.BlockSpec(memory_space=pltpu.VMEM) for _ in shapes],
        compiler_params=pltpu.CompilerParams(vmem_limit_bytes=min(2 * moved + (6 << 20), 40 << 20)),
        cost_estimate=pl.CostEstimate(flops=flops, bytes_accessed=moved, transcendentals=0),
    )(*args)


def unit(tokens):
    width = tokens.shape[1]
    centered = tokens - jnp.sum(tokens, axis=1, keepdims=True) / width
    inv_scale = lax.rsqrt(jnp.sum(centered * centered, axis=1, keepdims=True) / width + epsilon)
    return centered * inv_scale, inv_scale


def pack_body(tokens, cotangent, w_in, w_out, out, block):
    hidden = w_in.shape[1]
    block[0] = w_in[...]
    block[1, :hidden] = w_out[:, :hidden]
    block[1, hidden:] = w_out[:, hidden:]
    features = out.shape[2]
    normed = unit(tokens[...].astype(f32))[0]
    grads = cotangent[...].astype(f32)
    for part in range(ZH):
        cut = slice(part * features, (part + 1) * features)
        pair = jnp.concatenate([normed[:, cut], grads[:, cut]], axis=0).astype(bf16)
        out[part * ZL : (part + 1) * ZL] = jnp.broadcast_to(pair[None], (ZL,) + pair.shape)


def place(here, step, width):
    return pl.multiple_of(lax.rem(here + step, Y) * width, 128)


def hidden_body(here, rows, other, b0, b1, b3, far_in, far_out, out):
    width, hidden = far_in.shape
    pre = grad = None
    for step, (ins, cols) in enumerate(
        ((b0.at[0], b0.at[1]), (b1.at[0], b1.at[1]), (far_in, far_out), (b3.at[0], b3.at[1]))
    ):
        at = place(here[0], step, width)
        left = jnp.concatenate([rows[0, :, pl.ds(at, width)], other[0, :, pl.ds(at, width)]], axis=0)
        terms = [dot(left, ins[...])]
        for part in range(width // hidden):
            cut = pl.ds(pl.multiple_of(at + part * hidden, 128), hidden)
            right = jnp.concatenate([rows[1, :, cut], other[1, :, cut]], axis=0)
            terms.append(dot(right, cols[part * hidden : (part + 1) * hidden], LAST))
        one, two = terms[0], sum(terms[1:])
        pre = one if pre is None else pre + one
        grad = two if grad is None else grad + two
    pre, grad = pre.astype(bf16), grad.astype(bf16)
    for part in range(ZH):
        out[part, 0] = pre
        out[part, 1] = grad


def split_body(here, rows, other, *outs):
    half = rows.shape[1]
    width = outs[0].shape[2]
    for step, out in enumerate(outs):
        at = pl.ds(place(here[0], step, width), width)
        out[:, :half] = rows[:, :, at]
        out[:, half:] = other[:, :, at]


def output_body(here, parts, b0, b1, b3, far_in, far_out, pair, keep, give):
    width, hidden = far_in.shape
    half = keep.shape[1]
    value = parts[0, 0].astype(f32) + parts[1, 0].astype(f32)
    upstream = parts[0, 1].astype(f32) + parts[1, 1].astype(f32)
    square = value * value
    curve = jnp.tanh(RATE * (value + CUBE * (square * value)))
    chance = 0.5 * (1.0 + curve)
    slope = chance + 0.5 * value * (1.0 - curve * curve) * (RATE * (1.0 + 3.0 * CUBE * square))
    act = (value * chance).astype(bf16)
    pre_grad = (upstream * slope).astype(bf16)
    pair[0] = act
    pair[1] = pre_grad
    for step, (ins, cols) in enumerate(
        ((b0.at[0], b0.at[1]), (b1.at[0], b1.at[1]), (far_in, far_out), (b3.at[0], b3.at[1]))
    ):
        at = place(here[0], step, width)
        term = dot(pre_grad, ins[...], LAST)
        keep[1, :, pl.ds(at, width)] = term[:half]
        give[1, :, pl.ds(at, width)] = term[half:].astype(bf16)
        for part in range(width // hidden):
            cut = pl.ds(pl.multiple_of(at + part * hidden, 128), hidden)
            term = dot(act, cols[part * hidden : (part + 1) * hidden])
            keep[0, :, cut] = term[:half]
            give[0, :, cut] = term[half:].astype(bf16)


def weight_body(here, full, r0, r1, r2, r3, grad_w_in, grad_w_out):
    count = r0.shape[1]
    ins = outs = None
    for step, rows in enumerate((r0, r1, r2, r3)):
        at = pl.ds(pl.multiple_of(lax.rem(here[0] + Y - step, Y) * count, 128), count)
        one, two = dot(rows[0], full[1, at], FIRST), dot(full[0, at], rows[1], FIRST)
        ins = one if ins is None else ins + one
        outs = two if outs is None else outs + two
    grad_w_in[...] = ins
    grad_w_out[...] = outs


def final_body(tokens, cotangent, sums, mixed, grad_tokens):
    features = sums.shape[2]
    tokens_wide = tokens[...].astype(f32)
    unit_rows, inv_scale = unit(tokens_wide)
    halves = [
        jnp.sum(sums[part * ZL : (part + 1) * ZL].astype(f32), axis=0) for part in range(ZH)
    ]
    whole = jnp.concatenate(halves, axis=1)
    count = ZH * features
    mixed[...] = (tokens_wide + whole[0:1]).astype(bf16)
    normed_grad = whole[1:2]
    inner = jnp.sum(normed_grad * unit_rows, axis=1, keepdims=True) / count
    mean = jnp.sum(normed_grad, axis=1, keepdims=True) / count
    through = inv_scale * (normed_grad - mean - unit_rows * inner)
    grad_tokens[...] = (cotangent[...].astype(f32) + through).astype(bf16)


def local(tokens, w_in, w_out, cotangent):
    width, hidden = w_in.shape
    features = Y * width
    count = X * ZL * ZH * CORE
    half = count // CORE
    here = lax.axis_index("y").reshape(1).astype(jnp.int32)
    shape = jax.ShapeDtypeStruct
    work = 4 * count * features * hidden

    both, block = call(
        pack_body,
        [shape((ZH * ZL, 2, features), bf16), shape((2, width, hidden), bf16)],
        tokens, cotangent, w_in, w_out,
    )
    both, block = lax.optimization_barrier((both, block))
    both = trade(both, FAR).transpose(1, 0, 2)
    rows = lax.all_gather(both, "x", axis=1, tiled=True)
    other = swap(rows, "core")

    below, above = shift(block, "y", 1), shift(block, "y", -1)
    blocks = (block, above, below, shift(below[0], "y", 1), shift(above[1], "y", -1))

    (parts,) = call(hidden_body, [shape((ZH, 2, count, hidden), bf16)], here, rows, other, *blocks, flops=work)
    parts, rows, other = lax.optimization_barrier((parts, rows, other))
    parts = trade(parts, "zh")
    split = call(split_body, [shape((2, count, width), bf16)] * Y, here, rows, other)
    near = (shift(split[1], "y", 1), shift(split[3], "y", 3))
    parts, near = lax.optimization_barrier((parts, near))
    pair, keep, give = call(
        output_body,
        [shape((2, count, hidden), bf16), shape((2, half, features), f32), shape((2, half, features), bf16)],
        here, parts, *blocks, flops=work,
    )

    sums = keep + swap(give, "core").astype(f32)
    sums = sums.astype(bf16).reshape(2, X, half // X, features).transpose(1, 0, 2, 3)
    sums, pair = lax.optimization_barrier((sums, pair))
    sums, full = trade(sums, "x"), lax.all_gather(pair, "y", axis=1, tiled=True)
    sums, full = lax.optimization_barrier((sums, full))
    sums = total(sums).astype(bf16).transpose(1, 0, 2)
    sums, opposite = lax.optimization_barrier((sums, split[2]))
    sums = trade(sums, FAR)
    mixed, grad_tokens = call(
        final_body, [shape(tokens.shape, bf16)] * 2, tokens, cotangent, sums
    )

    spread = (split[0], near[0], shift(opposite, "y", 2), near[1])
    grad_w_in, grad_w_out = call(
        weight_body,
        [shape((width, hidden), f32), shape((hidden, width), f32)],
        here, full, *spread, flops=work,
    )
    return (mixed, grad_tokens, grad_w_in, grad_w_out)


def solution(mesh):
    fine = Mesh(mesh.devices.reshape(SIZES), AXES)
    dp, mp = ("zh", "y"), ("zl", "x", "core")
    return jax.shard_map(
        local,
        mesh=fine,
        in_specs=(P(dp + mp, None), P(dp, mp), P(mp, dp), P(dp + mp, None)),
        out_specs=(P(dp + mp, None), P(dp + mp, None), P(dp, mp), P(mp, dp)),
        check_vma=False,
    )
```

```python
import jax
import jax.numpy as jnp
from jax import lax
from jax.experimental import pallas as pl
from jax.experimental.pallas import tpu as pltpu
from jax.sharding import Mesh, PartitionSpec as P

epsilon = 1e-06
AXES = ("zh", "y", "zl", "x", "core")
SIZES = (2, 4, 8, 4, 2)
ZH, Y, ZL, X, CORE = SIZES
FAR = ("zh", "zl")
f32 = jnp.float32
bf16 = jnp.bfloat16
LAST = (((1,), (1,)), ((), ()))
FIRST = (((0,), (0,)), ((), ()))
RATE = 0.7978845608028654
CUBE = 0.044715


def swap(values, axis):
    return lax.ppermute(values, axis, [(0, 1), (1, 0)])


def shift(values, axis, step):
    count = lax.axis_size(axis)
    return lax.ppermute(values, axis, [(at, (at + step) % count) for at in range(count)])


def trade(values, axis):
    return lax.all_to_all(values, axis, split_axis=0, concat_axis=0, tiled=True)


def total(parts):
    return jnp.sum(parts.astype(f32), axis=0)


def dot(left, right, contract=(((1,), (0,)), ((), ()))):
    return lax.dot_general(left, right, contract, preferred_element_type=f32)


def call(body, shapes, *args, flops=0):
    moved = sum(a.size * a.dtype.itemsize for a in args) + sum(s.size * s.dtype.itemsize for s in shapes)
    specs = [
        pl.BlockSpec(memory_space=pltpu.SMEM if a.dtype == jnp.int32 else pltpu.VMEM) for a in args
    ]
    return pl.pallas_call(
        body,
        out_shape=shapes,
        in_specs=specs,
        out_specs=[pl.BlockSpec(memory_space=pltpu.VMEM) for _ in shapes],
        compiler_params=pltpu.CompilerParams(vmem_limit_bytes=min(2 * moved + (6 << 20), 40 << 20) if body is not pack_body else None),
        cost_estimate=pl.CostEstimate(flops=flops, bytes_accessed=moved, transcendentals=0),
    )(*args)


def unit(tokens):
    width = tokens.shape[1]
    centered = tokens - jnp.sum(tokens, axis=1, keepdims=True) / width
    inv_scale = lax.rsqrt(jnp.sum(centered * centered, axis=1, keepdims=True) / width + epsilon)
    return centered * inv_scale, inv_scale


def pack_body(tokens, cotangent, w_in, w_out, out, block):
    hidden = w_in.shape[1]
    block[0] = w_in[...]
    block[1, :hidden] = w_out[:, :hidden]
    block[1, hidden:] = w_out[:, hidden:]
    features = out.shape[2]
    normed = unit(tokens[...].astype(f32))[0]
    grads = cotangent[...].astype(f32)
    for part in range(ZH):
        cut = slice(part * features, (part + 1) * features)
        pair = jnp.concatenate([normed[:, cut], grads[:, cut]], axis=0).astype(bf16)
        out[part * ZL : (part + 1) * ZL] = jnp.broadcast_to(pair[None], (ZL,) + pair.shape)


def place(here, step, width):
    return pl.multiple_of(lax.rem(here + step, Y) * width, 128)


def line_up(rows, other, index, cut):
    return jnp.concatenate([ref[at, index, :, cut] for ref in (rows, other) for at in range(X)], axis=0)


def hidden_body(here, rows, other, b0, b1, b3, far_in, far_out, out):
    width, hidden = far_in.shape
    pre = grad = None
    for step, (ins, cols) in enumerate(
        ((b0.at[0], b0.at[1]), (b1.at[0], b1.at[1]), (far_in, far_out), (b3.at[0], b3.at[1]))
    ):
        at = place(here[0], step, width)
        left = line_up(rows, other, 0, pl.ds(at, width))
        terms = [dot(left, ins[...])]
        for part in range(width // hidden):
            cut = pl.ds(pl.multiple_of(at + part * hidden, 128), hidden)
            right = line_up(rows, other, 1, cut)
            terms.append(dot(right, cols[part * hidden : (part + 1) * hidden], LAST))
        one, two = terms[0], sum(terms[1:])
        pre = one if pre is None else pre + one
        grad = two if grad is None else grad + two
    pre, grad = pre.astype(bf16), grad.astype(bf16)
    for part in range(ZH):
        out[part, 0] = pre
        out[part, 1] = grad


def split_body(here, rows, other, *outs):
    width = outs[0].shape[2]
    for step, out in enumerate(outs):
        at = pl.ds(place(here[0], step, width), width)
        for index in range(2):
            out[index] = line_up(rows, other, index, at)


def output_body(here, parts, b0, b1, b3, far_in, far_out, pair, keep, give):
    width, hidden = far_in.shape
    half = keep.shape[1]
    value = parts[0, 0].astype(f32) + parts[1, 0].astype(f32)
    upstream = parts[0, 1].astype(f32) + parts[1, 1].astype(f32)
    square = value * value
    curve = jnp.tanh(RATE * (value + CUBE * (square * value)))
    chance = 0.5 * (1.0 + curve)
    slope = chance + 0.5 * value * (1.0 - curve * curve) * (RATE * (1.0 + 3.0 * CUBE * square))
    act = (value * chance).astype(bf16)
    pre_grad = (upstream * slope).astype(bf16)
    pair[0] = act
    pair[1] = pre_grad
    for step, (ins, cols) in enumerate(
        ((b0.at[0], b0.at[1]), (b1.at[0], b1.at[1]), (far_in, far_out), (b3.at[0], b3.at[1]))
    ):
        at = place(here[0], step, width)
        term = dot(pre_grad, ins[...], LAST)
        keep[1, :, pl.ds(at, width)] = term[:half]
        give[1, :, pl.ds(at, width)] = term[half:].astype(bf16)
        for part in range(width // hidden):
            cut = pl.ds(pl.multiple_of(at + part * hidden, 128), hidden)
            term = dot(act, cols[part * hidden : (part + 1) * hidden])
            keep[0, :, cut] = term[:half]
            give[0, :, cut] = term[half:].astype(bf16)


def weight_body(here, full, r0, r1, r2, r3, grad_w_in, grad_w_out):
    count = r0.shape[1]
    ins = outs = None
    for step, rows in enumerate((r0, r1, r2, r3)):
        at = pl.ds(pl.multiple_of(lax.rem(here[0] + Y - step, Y) * count, 128), count)
        one, two = dot(rows[0], full[1, at], FIRST), dot(full[0, at], rows[1], FIRST)
        ins = one if ins is None else ins + one
        outs = two if outs is None else outs + two
    grad_w_in[...] = ins
    grad_w_out[...] = outs


def final_body(tokens, cotangent, sums, mixed, grad_tokens):
    features = sums.shape[2]
    tokens_wide = tokens[...].astype(f32)
    unit_rows, inv_scale = unit(tokens_wide)
    halves = [
        jnp.sum(sums[part * ZL : (part + 1) * ZL].astype(f32), axis=0) for part in range(ZH)
    ]
    whole = jnp.concatenate(halves, axis=1)
    count = ZH * features
    mixed[...] = (tokens_wide + whole[0:1]).astype(bf16)
    normed_grad = whole[1:2]
    inner = jnp.sum(normed_grad * unit_rows, axis=1, keepdims=True) / count
    mean = jnp.sum(normed_grad, axis=1, keepdims=True) / count
    through = inv_scale * (normed_grad - mean - unit_rows * inner)
    grad_tokens[...] = (cotangent[...].astype(f32) + through).astype(bf16)


def local(tokens, w_in, w_out, cotangent):
    width, hidden = w_in.shape
    features = Y * width
    count = X * ZL * ZH * CORE
    half = count // CORE
    here = lax.axis_index("y").reshape(1).astype(jnp.int32)
    shape = jax.ShapeDtypeStruct
    work = 4 * count * features * hidden

    both, block = call(
        pack_body,
        [shape((ZH * ZL, 2, features), bf16), shape((2, width, hidden), bf16)],
        tokens, cotangent, w_in, w_out,
    )
    both, block = lax.optimization_barrier((both, block))
    below, above = shift(block, "y", 1), shift(block, "y", -1)
    both, near_in, near_out = lax.optimization_barrier((trade(both, FAR), below[0], above[1]))
    both = both.transpose(1, 0, 2)
    rows = trade(jnp.broadcast_to(both, (X,) + both.shape), "x")
    far_in, far_out = shift(near_in, "y", 1), shift(near_out, "y", -1)
    rows, far_in, far_out = lax.optimization_barrier((rows, far_in, far_out))
    other = swap(rows, "core")
    blocks = (block, above, below, far_in, far_out)

    (parts,) = call(hidden_body, [shape((ZH, 2, count, hidden), bf16)], here, rows, other, *blocks, flops=work)
    parts, rows, other = lax.optimization_barrier((parts, rows, other))
    parts = trade(parts, "zh")
    split = call(split_body, [shape((2, count, width), bf16)] * Y, here, rows, other)
    near = (shift(split[1], "y", 1), shift(split[3], "y", 3))
    parts, near = lax.optimization_barrier((parts, near))
    pair, keep, give = call(
        output_body,
        [shape((2, count, hidden), bf16), shape((2, half, features), f32), shape((2, half, features), bf16)],
        here, parts, *blocks, flops=work,
    )

    sums = keep + swap(give, "core").astype(f32)
    sums = sums.astype(bf16).reshape(2, X, half // X, features).transpose(1, 0, 2, 3)
    sums, pair = lax.optimization_barrier((sums, pair))
    sums, full = trade(sums, "x"), lax.all_gather(pair, "y", axis=1, tiled=True)
    sums, full = lax.optimization_barrier((sums, full))
    sums = total(sums).astype(bf16).transpose(1, 0, 2)
    sums, opposite = lax.optimization_barrier((sums, split[2]))
    sums = trade(sums, FAR)
    mixed, grad_tokens = call(
        final_body, [shape(tokens.shape, bf16)] * 2, tokens, cotangent, sums
    )

    spread = (split[0], near[0], shift(opposite, "y", 2), near[1])
    grad_w_in, grad_w_out = call(
        weight_body,
        [shape((width, hidden), f32), shape((hidden, width), f32)],
        here, full, *spread, flops=work,
    )
    return (mixed, grad_tokens, grad_w_in, grad_w_out)


def solution(mesh):
    fine = Mesh(mesh.devices.reshape(SIZES), AXES)
    dp, mp = ("zh", "y"), ("zl", "x", "core")
    return jax.shard_map(
        local,
        mesh=fine,
        in_specs=(P(dp + mp, None), P(dp, mp), P(mp, dp), P(dp + mp, None)),
        out_specs=(P(dp + mp, None), P(dp + mp, None), P(dp, mp), P(mp, dp)),
        check_vma=False,
    )
```

```python
import jax
import jax.numpy as jnp
from jax import lax
from jax.experimental import pallas as pl
from jax.experimental.pallas import tpu as pltpu
from jax.sharding import Mesh, PartitionSpec as P

epsilon = 1e-06
AXES = ("zh", "y", "zl", "x", "core")
SIZES = (2, 4, 8, 4, 2)
ZH, Y, ZL, X, CORE = SIZES
FAR = ("zh", "zl")
f32 = jnp.float32
bf16 = jnp.bfloat16
LAST = (((1,), (1,)), ((), ()))
FIRST = (((0,), (0,)), ((), ()))
RATE = 0.7978845608028654
CUBE = 0.044715


def swap(values, axis):
    return lax.ppermute(values, axis, [(0, 1), (1, 0)])


def shift(values, axis, step):
    count = lax.axis_size(axis)
    return lax.ppermute(values, axis, [(at, (at + step) % count) for at in range(count)])


def trade(values, axis):
    return lax.all_to_all(values, axis, split_axis=0, concat_axis=0, tiled=True)


def dot(left, right, contract=(((1,), (0,)), ((), ()))):
    return lax.dot_general(left, right, contract, preferred_element_type=f32)


def call(body, shapes, *args, flops=0):
    moved = sum(a.size * a.dtype.itemsize for a in args) + sum(s.size * s.dtype.itemsize for s in shapes)
    specs = [
        pl.BlockSpec(memory_space=pltpu.SMEM if a.dtype == jnp.int32 else pltpu.VMEM) for a in args
    ]
    return pl.pallas_call(
        body,
        out_shape=shapes,
        in_specs=specs,
        out_specs=[pl.BlockSpec(memory_space=pltpu.VMEM) for _ in shapes],
        compiler_params=pltpu.CompilerParams(vmem_limit_bytes=min(2 * moved + (6 << 20), 40 << 20) if body is not pack_body else None),
        cost_estimate=pl.CostEstimate(flops=flops, bytes_accessed=moved, transcendentals=0),
    )(*args)


def unit(tokens):
    width = tokens.shape[1]
    centered = tokens - jnp.sum(tokens, axis=1, keepdims=True) / width
    inv_scale = lax.rsqrt(jnp.sum(centered * centered, axis=1, keepdims=True) / width + epsilon)
    return centered * inv_scale, inv_scale


def pack_body(tokens, cotangent, w_in, w_out, out, block):
    hidden = w_in.shape[1]
    block[0] = w_in[...]
    block[1, :hidden] = w_out[:, :hidden]
    block[1, hidden:] = w_out[:, hidden:]
    features = out.shape[2]
    normed = unit(tokens[...].astype(f32))[0]
    grads = cotangent[...].astype(f32)
    for part in range(ZH):
        cut = slice(part * features, (part + 1) * features)
        pair = jnp.concatenate([normed[:, cut], grads[:, cut]], axis=0).astype(bf16)
        out[part * ZL : (part + 1) * ZL] = jnp.broadcast_to(pair[None], (ZL,) + pair.shape)


def place(here, step, width):
    return pl.multiple_of(lax.rem(here + step, Y) * width, 128)


def line_up(rows, other, index, cut):
    return jnp.concatenate([ref[at, index, :, cut] for ref in (rows, other) for at in range(X)], axis=0)


def hidden_body(here, rows, other, b0, b1, b3, far_in, far_out, out):
    width, hidden = far_in.shape
    pre = grad = None
    for step, (ins, cols) in enumerate(
        ((b0.at[0], b0.at[1]), (b1.at[0], b1.at[1]), (far_in, far_out), (b3.at[0], b3.at[1]))
    ):
        at = place(here[0], step, width)
        left = line_up(rows, other, 0, pl.ds(at, width))
        terms = [dot(left, ins[...])]
        for part in range(width // hidden):
            cut = pl.ds(pl.multiple_of(at + part * hidden, 128), hidden)
            right = line_up(rows, other, 1, cut)
            terms.append(dot(right, cols[part * hidden : (part + 1) * hidden], LAST))
        one, two = terms[0], sum(terms[1:])
        pre = one if pre is None else pre + one
        grad = two if grad is None else grad + two
    out[0] = pre.astype(bf16)
    out[1] = grad.astype(bf16)


def split_body(rows, other, out):
    width = out.shape[3]
    for step in range(Y):
        for index in range(2):
            out[step, index] = line_up(rows, other, index, slice(step * width, (step + 1) * width))


def output_body(here, parts, far, b0, b1, b3, far_in, far_out, pair, keep, give):
    width, hidden = far_in.shape
    half = keep.shape[1]
    value = parts[0].astype(f32) + far[0].astype(f32)
    upstream = parts[1].astype(f32) + far[1].astype(f32)
    square = value * value
    curve = jnp.tanh(RATE * (value + CUBE * (square * value)))
    chance = 0.5 * (1.0 + curve)
    slope = chance + 0.5 * value * (1.0 - curve * curve) * (RATE * (1.0 + 3.0 * CUBE * square))
    act = (value * chance).astype(bf16)
    pre_grad = (upstream * slope).astype(bf16)
    pair[0] = act
    pair[1] = pre_grad
    for step, (ins, cols) in enumerate(
        ((b0.at[0], b0.at[1]), (b1.at[0], b1.at[1]), (far_in, far_out), (b3.at[0], b3.at[1]))
    ):
        at = place(here[0], step, width)
        term = dot(pre_grad, ins[...], LAST)
        keep[1, :, pl.ds(at, width)] = term[:half]
        give[1, :, pl.ds(at, width)] = term[half:].astype(bf16)
        for part in range(width // hidden):
            cut = pl.ds(pl.multiple_of(at + part * hidden, 128), hidden)
            term = dot(act, cols[part * hidden : (part + 1) * hidden])
            keep[0, :, cut] = term[:half]
            give[0, :, cut] = term[half:].astype(bf16)


def weight_body(full, rows, grad_w_in, grad_w_out):
    count = rows.shape[2]
    ins = outs = None
    for step in range(Y):
        at = slice(step * count, (step + 1) * count)
        one, two = dot(rows[step, 0], full[1, at], FIRST), dot(full[0, at], rows[step, 1], FIRST)
        ins = one if ins is None else ins + one
        outs = two if outs is None else outs + two
    grad_w_in[...] = ins
    grad_w_out[...] = outs


def add_body(keep, far, out):
    rows = out.shape[2]
    for step in range(X):
        at = slice(step * rows, (step + 1) * rows)
        out[step] = (keep[:, at] + far[:, at].astype(f32)).astype(bf16)


def sum_body(parts, out):
    first, second = (
        sum(parts[step, index].astype(f32) for step in range(X)).astype(bf16).astype(f32) for index in range(2)
    )
    for row in range(out.shape[0]):
        cut = slice(row, row + 1)
        out[row] = jnp.concatenate([first[cut], second[cut]], axis=0).astype(bf16)


def final_body(tokens, cotangent, sums, mixed, grad_tokens):
    features = sums.shape[2]
    tokens_wide = tokens[...].astype(f32)
    unit_rows, inv_scale = unit(tokens_wide)
    halves = [
        jnp.sum(sums[part * ZL : (part + 1) * ZL].astype(f32), axis=0) for part in range(ZH)
    ]
    whole = jnp.concatenate(halves, axis=1)
    count = ZH * features
    mixed[...] = (tokens_wide + whole[0:1]).astype(bf16)
    normed_grad = whole[1:2]
    inner = jnp.sum(normed_grad * unit_rows, axis=1, keepdims=True) / count
    mean = jnp.sum(normed_grad, axis=1, keepdims=True) / count
    through = inv_scale * (normed_grad - mean - unit_rows * inner)
    grad_tokens[...] = (cotangent[...].astype(f32) + through).astype(bf16)


def local(tokens, w_in, w_out, cotangent):
    width, hidden = w_in.shape
    features = Y * width
    count = X * ZL * ZH * CORE
    half = count // CORE
    here = lax.axis_index("y").reshape(1).astype(jnp.int32)
    shape = jax.ShapeDtypeStruct
    work = 4 * count * features * hidden

    both, block = call(
        pack_body,
        [shape((ZH * ZL, 2, features), bf16), shape((2, width, hidden), bf16)],
        tokens, cotangent, w_in, w_out,
    )
    both, block = lax.optimization_barrier((both, block))
    below, above = shift(block, "y", 1), shift(block, "y", -1)
    both, near_in, near_out = lax.optimization_barrier((trade(both, FAR), below[0], above[1]))
    both = both.transpose(1, 0, 2)
    rows = trade(jnp.broadcast_to(both, (X,) + both.shape), "x")
    far_in, far_out = shift(near_in, "y", 1), shift(near_out, "y", -1)
    rows, far_in, far_out = lax.optimization_barrier((rows, far_in, far_out))
    other = swap(rows, "core")
    blocks = (block, above, below, far_in, far_out)

    (parts,) = call(hidden_body, [shape((2, count, hidden), bf16)], here, rows, other, *blocks, flops=work)
    parts, rows, other = lax.optimization_barrier((parts, rows, other))
    far = swap(parts, "zh")
    (spread,) = call(split_body, [shape((Y, 2, count, width), bf16)], rows, other)
    far, spread = lax.optimization_barrier((far, trade(spread, "y")))
    pair, keep, give = call(
        output_body,
        [shape((2, count, hidden), bf16), shape((2, half, features), f32), shape((2, half, features), bf16)],
        here, parts, far, *blocks, flops=work,
    )

    (sums,) = call(add_body, [shape((X, 2, half // X, features), bf16)], keep, swap(give, "core"))
    sums, pair = lax.optimization_barrier((sums, pair))
    sums, full = lax.optimization_barrier((trade(sums, "x"), lax.all_gather(pair, "y", axis=1, tiled=True)))
    (sums,) = call(sum_body, [shape((half // X, 2, features), bf16)], sums)
    sums = trade(sums, FAR)
    mixed, grad_tokens = call(
        final_body, [shape(tokens.shape, bf16)] * 2, tokens, cotangent, sums
    )

    grad_w_in, grad_w_out = call(
        weight_body,
        [shape((width, hidden), f32), shape((hidden, width), f32)],
        full, spread, flops=work,
    )
    return (mixed, grad_tokens, grad_w_in, grad_w_out)


def solution(mesh):
    fine = Mesh(mesh.devices.reshape(SIZES), AXES)
    dp, mp = ("zh", "y"), ("zl", "x", "core")
    return jax.shard_map(
        local,
        mesh=fine,
        in_specs=(P(dp + mp, None), P(dp, mp), P(mp, dp), P(dp + mp, None)),
        out_specs=(P(dp + mp, None), P(dp + mp, None), P(dp, mp), P(mp, dp)),
        check_vma=False,
    )
```

```python
import jax
import jax.numpy as jnp
from jax import lax
from jax.experimental import pallas as pl
from jax.experimental.pallas import tpu as pltpu
from jax.sharding import Mesh, PartitionSpec as P

epsilon = 1e-06
AXES = ("zh", "y", "zl", "x", "core")
SIZES = (2, 4, 8, 4, 2)
ZH, Y, ZL, X, CORE = SIZES
FAR = ("zh", "zl")
f32 = jnp.float32
bf16 = jnp.bfloat16
LAST = (((1,), (1,)), ((), ()))
FIRST = (((0,), (0,)), ((), ()))
RATE = 0.7978845608028654
CUBE = 0.044715


def swap(values, axis):
    return lax.ppermute(values, axis, [(0, 1), (1, 0)])


def shift(values, axis, step):
    count = lax.axis_size(axis)
    return lax.ppermute(values, axis, [(at, (at + step) % count) for at in range(count)])


def trade(values, axis):
    return lax.all_to_all(values, axis, split_axis=0, concat_axis=0, tiled=True)


def dot(left, right, contract=(((1,), (0,)), ((), ()))):
    return lax.dot_general(left, right, contract, preferred_element_type=f32)


def call(body, shapes, *args, flops=0):
    moved = sum(a.size * a.dtype.itemsize for a in args) + sum(s.size * s.dtype.itemsize for s in shapes)
    specs = [
        pl.BlockSpec(memory_space=pltpu.SMEM if a.dtype == jnp.int32 else pltpu.VMEM) for a in args
    ]
    return pl.pallas_call(
        body,
        out_shape=shapes,
        in_specs=specs,
        out_specs=[pl.BlockSpec(memory_space=pltpu.VMEM) for _ in shapes],
        compiler_params=pltpu.CompilerParams(vmem_limit_bytes=min(2 * moved + (6 << 20), 40 << 20) if body is not pack_body else None),
        cost_estimate=pl.CostEstimate(flops=flops, bytes_accessed=moved, transcendentals=0),
    )(*args)


def unit(tokens):
    width = tokens.shape[1]
    centered = tokens - jnp.sum(tokens, axis=1, keepdims=True) / width
    inv_scale = lax.rsqrt(jnp.sum(centered * centered, axis=1, keepdims=True) / width + epsilon)
    return centered * inv_scale, inv_scale


def pack_body(tokens, cotangent, w_in, w_out, out, block):
    hidden = w_in.shape[1]
    block[0] = w_in[...]
    block[1, :hidden] = w_out[:, :hidden]
    block[1, hidden:] = w_out[:, hidden:]
    features = out.shape[2]
    normed = unit(tokens[...].astype(f32))[0]
    grads = cotangent[...].astype(f32)
    for part in range(ZH):
        cut = slice(part * features, (part + 1) * features)
        pair = jnp.concatenate([normed[:, cut], grads[:, cut]], axis=0).astype(bf16)
        out[part * ZL : (part + 1) * ZL] = jnp.broadcast_to(pair[None], (ZL,) + pair.shape)


def place(here, step, width):
    return pl.multiple_of(lax.rem(here + step, Y) * width, 128)


def line_up(rows, other, index, cut):
    return jnp.concatenate([ref[at, index, :, cut] for ref in (rows, other) for at in range(X)], axis=0)


def hidden_body(here, rows, other, b0, b1, b3, far_in, far_out, out):
    width, hidden = far_in.shape
    pre = grad = None
    for step, (ins, cols) in enumerate(
        ((b0.at[0], b0.at[1]), (b1.at[0], b1.at[1]), (far_in, far_out), (b3.at[0], b3.at[1]))
    ):
        at = place(here[0], step, width)
        left = line_up(rows, other, 0, pl.ds(at, width))
        terms = [dot(left, ins[...])]
        for part in range(width // hidden):
            cut = pl.ds(pl.multiple_of(at + part * hidden, 128), hidden)
            right = line_up(rows, other, 1, cut)
            terms.append(dot(right, cols[part * hidden : (part + 1) * hidden], LAST))
        one, two = terms[0], sum(terms[1:])
        pre = one if pre is None else pre + one
        grad = two if grad is None else grad + two
    out[0] = pre.astype(bf16)
    out[1] = grad.astype(bf16)


def split_body(rows, out):
    width = out.shape[3]
    for step in range(Y):
        for index in range(2):
            cut = slice(step * width, (step + 1) * width)
            out[step, index] = jnp.concatenate([rows[at, index, :, cut] for at in range(X)], axis=0)


def output_body(here, parts, b0, b1, b3, far_in, far_out, pair, keep, give):
    width, hidden = far_in.shape
    half = keep.shape[1]
    value = parts[0, 0].astype(f32) + parts[1, 0].astype(f32)
    upstream = parts[0, 1].astype(f32) + parts[1, 1].astype(f32)
    square = value * value
    curve = jnp.tanh(RATE * (value + CUBE * (square * value)))
    chance = 0.5 * (1.0 + curve)
    slope = chance + 0.5 * value * (1.0 - curve * curve) * (RATE * (1.0 + 3.0 * CUBE * square))
    act = (value * chance).astype(bf16)
    pre_grad = (upstream * slope).astype(bf16)
    pair[0] = act
    pair[1] = pre_grad
    for step, (ins, cols) in enumerate(
        ((b0.at[0], b0.at[1]), (b1.at[0], b1.at[1]), (far_in, far_out), (b3.at[0], b3.at[1]))
    ):
        at = place(here[0], step, width)
        term = dot(pre_grad, ins[...], LAST)
        keep[1, :, pl.ds(at, width)] = term[:half]
        give[1, :, pl.ds(at, width)] = term[half:].astype(bf16)
        for part in range(width // hidden):
            cut = pl.ds(pl.multiple_of(at + part * hidden, 128), hidden)
            term = dot(act, cols[part * hidden : (part + 1) * hidden])
            keep[0, :, cut] = term[:half]
            give[0, :, cut] = term[half:].astype(bf16)


def weight_body(full, mine, theirs, grad_w_in, grad_w_out):
    count = mine.shape[2]
    ins = outs = None
    for step in range(Y * CORE):
        at = slice(step * count, (step + 1) * count)
        rows = (mine, theirs)[step % CORE].at[step // CORE]
        one, two = dot(rows[0], full[1, at], FIRST), dot(full[0, at], rows[1], FIRST)
        ins = one if ins is None else ins + one
        outs = two if outs is None else outs + two
    grad_w_in[...] = ins
    grad_w_out[...] = outs


def add_body(keep, far, out):
    rows = out.shape[2]
    for step in range(X):
        at = slice(step * rows, (step + 1) * rows)
        out[step] = (keep[:, at] + far[:, at].astype(f32)).astype(bf16)


def sum_body(parts, out):
    first, second = (
        sum(parts[step, index].astype(f32) for step in range(X)).astype(bf16).astype(f32) for index in range(2)
    )
    for row in range(out.shape[0]):
        cut = slice(row, row + 1)
        out[row] = jnp.concatenate([first[cut], second[cut]], axis=0).astype(bf16)


def final_body(tokens, cotangent, sums, mixed, grad_tokens):
    features = sums.shape[2]
    tokens_wide = tokens[...].astype(f32)
    unit_rows, inv_scale = unit(tokens_wide)
    halves = [
        jnp.sum(sums[part * ZL : (part + 1) * ZL].astype(f32), axis=0) for part in range(ZH)
    ]
    whole = jnp.concatenate(halves, axis=1)
    count = ZH * features
    mixed[...] = (tokens_wide + whole[0:1]).astype(bf16)
    normed_grad = whole[1:2]
    inner = jnp.sum(normed_grad * unit_rows, axis=1, keepdims=True) / count
    mean = jnp.sum(normed_grad, axis=1, keepdims=True) / count
    through = inv_scale * (normed_grad - mean - unit_rows * inner)
    grad_tokens[...] = (cotangent[...].astype(f32) + through).astype(bf16)


def local(tokens, w_in, w_out, cotangent):
    width, hidden = w_in.shape
    features = Y * width
    count = X * ZL * ZH * CORE
    half = count // CORE
    here = lax.axis_index("y").reshape(1).astype(jnp.int32)
    shape = jax.ShapeDtypeStruct
    work = 4 * count * features * hidden

    both, block = call(
        pack_body,
        [shape((ZH * ZL, 2, features), bf16), shape((2, width, hidden), bf16)],
        tokens, cotangent, w_in, w_out,
    )
    both, block = lax.optimization_barrier((both, block))
    below, above = shift(block, "y", 1), shift(block, "y", -1)
    both, near_in, near_out = lax.optimization_barrier((trade(both, FAR), below[0], above[1]))
    both = both.transpose(1, 0, 2)
    rows = trade(jnp.broadcast_to(both, (X,) + both.shape), "x")
    far_in, far_out = shift(near_in, "y", 1), shift(near_out, "y", -1)
    (mine,) = call(split_body, [shape((Y, 2, half, width), bf16)], rows)
    rows, far_in, far_out, mine = lax.optimization_barrier((rows, far_in, far_out, mine))
    other = swap(rows, "core")
    mine = trade(mine, "y")
    blocks = (block, above, below, far_in, far_out)

    (parts,) = call(hidden_body, [shape((2, count, hidden), bf16)], here, rows, other, *blocks, flops=work)
    parts, mine = lax.optimization_barrier((lax.all_gather(parts, "zh"), mine))
    pair, keep, give = call(
        output_body,
        [shape((2, count, hidden), bf16), shape((2, half, features), f32), shape((2, half, features), bf16)],
        here, parts, *blocks, flops=work,
    )

    (sums,) = call(add_body, [shape((X, 2, half // X, features), bf16)], keep, swap(give, "core"))
    sums, pair, mine = lax.optimization_barrier((sums, pair, mine))
    full = lax.all_gather(pair, "y", axis=1, tiled=True)
    sums, full, theirs = lax.optimization_barrier((trade(sums, "x"), full, swap(mine, "core")))
    (sums,) = call(sum_body, [shape((half // X, 2, features), bf16)], sums)
    sums = trade(sums, FAR)

    grad_w_in, grad_w_out = call(
        weight_body,
        [shape((width, hidden), f32), shape((hidden, width), f32)],
        full, mine, theirs, flops=work,
    )

    sums, grad_w_in, grad_w_out = lax.optimization_barrier((sums, grad_w_in, grad_w_out))
    mixed, grad_tokens = call(
        final_body, [shape(tokens.shape, bf16)] * 2, tokens, cotangent, sums
    )
    return (mixed, grad_tokens, grad_w_in, grad_w_out)


def solution(mesh):
    fine = Mesh(mesh.devices.reshape(SIZES), AXES)
    dp, mp = ("zh", "y"), ("zl", "x", "core")
    return jax.shard_map(
        local,
        mesh=fine,
        in_specs=(P(dp + mp, None), P(dp, mp), P(mp, dp), P(dp + mp, None)),
        out_specs=(P(dp + mp, None), P(dp + mp, None), P(dp, mp), P(mp, dp)),
        check_vma=False,
    )
```

```python
import jax
import jax.numpy as jnp
from jax import lax
from jax.experimental import pallas as pl
from jax.experimental.pallas import tpu as pltpu
from jax.sharding import Mesh, PartitionSpec as P

epsilon = 1e-06
AXES = ("zh", "y", "zl", "x", "core")
SIZES = (2, 4, 8, 4, 2)
ZH, Y, ZL, X, CORE = SIZES
FAR = ("zh", "zl")
f32 = jnp.float32
bf16 = jnp.bfloat16
LAST = (((1,), (1,)), ((), ()))
FIRST = (((0,), (0,)), ((), ()))
RATE = 0.7978845608028654
CUBE = 0.044715


def swap(values, axis):
    return lax.ppermute(values, axis, [(0, 1), (1, 0)])


def shift(values, axis, step):
    count = lax.axis_size(axis)
    return lax.ppermute(values, axis, [(at, (at + step) % count) for at in range(count)])


def trade(values, axis):
    return lax.all_to_all(values, axis, split_axis=0, concat_axis=0, tiled=True)


def dot(left, right, contract=(((1,), (0,)), ((), ()))):
    return lax.dot_general(left, right, contract, preferred_element_type=f32)


def call(body, shapes, *args, flops=0):
    moved = sum(a.size * a.dtype.itemsize for a in args) + sum(s.size * s.dtype.itemsize for s in shapes)
    specs = [
        pl.BlockSpec(memory_space=pltpu.SMEM if a.dtype == jnp.int32 else pltpu.VMEM) for a in args
    ]
    return pl.pallas_call(
        body,
        out_shape=shapes,
        in_specs=specs,
        out_specs=[pl.BlockSpec(memory_space=pltpu.VMEM) for _ in shapes],
        compiler_params=pltpu.CompilerParams(vmem_limit_bytes=(moved + (4 << 20)) if len(args) < 6 else None),
        cost_estimate=pl.CostEstimate(flops=flops, bytes_accessed=moved, transcendentals=0),
    )(*args)


def unit(tokens):
    width = tokens.shape[1]
    centered = tokens - jnp.sum(tokens, axis=1, keepdims=True) / width
    inv_scale = lax.rsqrt(jnp.sum(centered * centered, axis=1, keepdims=True) / width + epsilon)
    return centered * inv_scale, inv_scale


def pack_body(tokens, cotangent, out):
    features = out.shape[2]
    normed = unit(tokens[...].astype(f32))[0]
    grads = cotangent[...].astype(f32)
    for part in range(ZH):
        cut = slice(part * features, (part + 1) * features)
        pair = jnp.concatenate([normed[:, cut], grads[:, cut]], axis=0).astype(bf16)
        out[part * ZL : (part + 1) * ZL] = jnp.broadcast_to(pair[None], (ZL,) + pair.shape)


def place(here, step, width):
    return pl.multiple_of(lax.rem(here + step, Y) * width, 128)


def line_up(rows, other, index, cut):
    return jnp.concatenate([ref[at, index, :, cut] for ref in (rows, other) for at in range(X)], axis=0)


def hidden_body(here, rows, other, i0, i1, i2, i3, o0, o1, o2, o3, out):
    width = i0.shape[0]
    pre = grad = None
    for step, (ins, outs) in enumerate(((i0, o0), (i1, o1), (i2, o2), (i3, o3))):
        at = pl.ds(place(here[0], step, width), width)
        one = dot(line_up(rows, other, 0, at), ins[...])
        two = dot(line_up(rows, other, 1, at), outs[...], LAST)
        pre = one if pre is None else pre + one
        grad = two if grad is None else grad + two
    out[0] = pre.astype(bf16)
    out[1] = grad.astype(bf16)


def split_body(rows, out):
    width = out.shape[3]
    for step in range(Y):
        for index in range(2):
            cut = slice(step * width, (step + 1) * width)
            out[step, index] = jnp.concatenate([rows[at, index, :, cut] for at in range(X)], axis=0)


def output_body(here, parts, i0, i1, i2, i3, o0, o1, o2, o3, pair, keep, give):
    width = i0.shape[0]
    half = keep.shape[1]
    value = parts[0, 0].astype(f32) + parts[1, 0].astype(f32)
    upstream = parts[0, 1].astype(f32) + parts[1, 1].astype(f32)
    square = value * value
    curve = jnp.tanh(RATE * (value + CUBE * (square * value)))
    chance = 0.5 * (1.0 + curve)
    slope = chance + 0.5 * value * (1.0 - curve * curve) * (RATE * (1.0 + 3.0 * CUBE * square))
    act = (value * chance).astype(bf16)
    pre_grad = (upstream * slope).astype(bf16)
    pair[0] = act
    pair[1] = pre_grad
    for step, (ins, outs) in enumerate(((i0, o0), (i1, o1), (i2, o2), (i3, o3))):
        at = pl.ds(place(here[0], step, width), width)
        for index, term in enumerate((dot(act, outs[...]), dot(pre_grad, ins[...], LAST))):
            keep[index, :, at] = term[:half]
            give[index, :, at] = term[half:].astype(bf16)


def weight_body(full, mine, theirs, grad_w_in, grad_w_out):
    def every(index):
        return jnp.concatenate([ref[step, index] for step in range(Y) for ref in (mine, theirs)], axis=0)

    grad_w_in[...] = dot(every(0), full[1], FIRST)
    grad_w_out[...] = dot(full[0], every(1), FIRST)


def add_body(keep, far, out):
    rows = out.shape[2]
    for step in range(X):
        at = slice(step * rows, (step + 1) * rows)
        out[step] = (keep[:, at] + far[:, at].astype(f32)).astype(bf16)


def sum_body(parts, out):
    first, second = (
        sum(parts[step, index].astype(f32) for step in range(X)).astype(bf16).astype(f32) for index in range(2)
    )
    for row in range(out.shape[0]):
        cut = slice(row, row + 1)
        out[row] = jnp.concatenate([first[cut], second[cut]], axis=0).astype(bf16)


def final_body(tokens, cotangent, sums, mixed, grad_tokens):
    features = sums.shape[2]
    tokens_wide = tokens[...].astype(f32)
    unit_rows, inv_scale = unit(tokens_wide)
    halves = [
        jnp.sum(sums[part * ZL : (part + 1) * ZL].astype(f32), axis=0) for part in range(ZH)
    ]
    whole = jnp.concatenate(halves, axis=1)
    count = ZH * features
    mixed[...] = (tokens_wide + whole[0:1]).astype(bf16)
    normed_grad = whole[1:2]
    inner = jnp.sum(normed_grad * unit_rows, axis=1, keepdims=True) / count
    mean = jnp.sum(normed_grad, axis=1, keepdims=True) / count
    through = inv_scale * (normed_grad - mean - unit_rows * inner)
    grad_tokens[...] = (cotangent[...].astype(f32) + through).astype(bf16)


def local(tokens, w_in, w_out, cotangent):
    width, hidden = w_in.shape
    features = Y * width
    count = X * ZL * ZH * CORE
    half = count // CORE
    here = lax.axis_index("y").reshape(1).astype(jnp.int32)
    shape = jax.ShapeDtypeStruct
    work = 4 * count * features * hidden

    (both,) = call(pack_body, [shape((ZH * ZL, 2, features), bf16)], tokens, cotangent)
    both, w_in_sent, w_out_sent = lax.optimization_barrier((both, w_in, w_out))
    i3, o1 = shift(w_in_sent, "y", 1), shift(w_out_sent, "y", -1)
    i2, o2 = shift(i3, "y", 1), shift(o1, "y", -1)
    both, i2, o2, w_in_sent, w_out_sent = lax.optimization_barrier(
        (trade(both, FAR), i2, o2, w_in_sent, w_out_sent)
    )
    both = both.transpose(1, 0, 2)
    rows = trade(jnp.broadcast_to(both, (X,) + both.shape), "x")
    i1, o3 = shift(w_in_sent, "y", -1), shift(w_out_sent, "y", 1)
    (mine,) = call(split_body, [shape((Y, 2, half, width), bf16)], rows)
    rows, i1, o3, mine = lax.optimization_barrier((rows, i1, o3, mine))
    other = swap(rows, "core")
    mine = trade(mine, "y")
    blocks = (w_in, i1, i2, i3, w_out, o1, o2, o3)

    (parts,) = call(hidden_body, [shape((2, count, hidden), bf16)], here, rows, other, *blocks, flops=work)
    parts, mine = lax.optimization_barrier((lax.all_gather(parts, "zh"), mine))
    pair, keep, give = call(
        output_body,
        [shape((2, count, hidden), bf16), shape((2, half, features), f32), shape((2, half, features), bf16)],
        here, parts, *blocks, flops=work,
    )

    (sums,) = call(add_body, [shape((X, 2, half // X, features), bf16)], keep, swap(give, "core"))
    sums, pair, mine = lax.optimization_barrier((sums, pair, mine))
    full = lax.all_gather(pair, "y", axis=1, tiled=True)
    sums, full, theirs = lax.optimization_barrier((trade(sums, "x"), full, swap(mine, "core")))
    (sums,) = call(sum_body, [shape((half // X, 2, features), bf16)], sums)
    sums = trade(sums, FAR)

    grad_w_in, grad_w_out = call(
        weight_body,
        [shape((width, hidden), f32), shape((hidden, width), f32)],
        full, mine, theirs, flops=work,
    )

    sums, grad_w_in, grad_w_out = lax.optimization_barrier((sums, grad_w_in, grad_w_out))
    mixed, grad_tokens = call(
        final_body, [shape(tokens.shape, bf16)] * 2, tokens, cotangent, sums
    )
    return (mixed, grad_tokens, grad_w_in, grad_w_out)


def solution(mesh):
    fine = Mesh(mesh.devices.reshape(SIZES), AXES)
    dp, mp = ("zh", "y"), ("zl", "x", "core")
    return jax.shard_map(
        local,
        mesh=fine,
        in_specs=(P(dp + mp, None), P(dp, mp), P(mp, dp), P(dp + mp, None)),
        out_specs=(P(dp + mp, None), P(dp + mp, None), P(dp, mp), P(mp, dp)),
        check_vma=False,
    )
```

```python
import jax
import jax.numpy as jnp
from jax import lax
from jax.experimental import pallas as pl
from jax.experimental.pallas import tpu as pltpu
from jax.sharding import Mesh, PartitionSpec as P

epsilon = 1e-06
AXES = ("zh", "y", "zl", "x", "core")
SIZES = (2, 4, 8, 4, 2)
ZH, Y, ZL, X, CORE = SIZES
FAR = ("zh", "zl")
f32 = jnp.float32
bf16 = jnp.bfloat16
LAST = (((1,), (1,)), ((), ()))
FIRST = (((0,), (0,)), ((), ()))
RATE = 0.7978845608028654
CUBE = 0.044715


def swap(values, axis):
    return lax.ppermute(values, axis, [(0, 1), (1, 0)])


def shift(values, axis, step):
    count = lax.axis_size(axis)
    return lax.ppermute(values, axis, [(at, (at + step) % count) for at in range(count)])


def trade(values, axis):
    return lax.all_to_all(values, axis, split_axis=0, concat_axis=0, tiled=True)


def dot(left, right, contract=(((1,), (0,)), ((), ()))):
    return lax.dot_general(left, right, contract, preferred_element_type=f32)


def call(body, shapes, *args, flops=0):
    moved = sum(a.size * a.dtype.itemsize for a in args) + sum(s.size * s.dtype.itemsize for s in shapes)
    specs = [
        pl.BlockSpec(memory_space=pltpu.SMEM if a.dtype == jnp.int32 else pltpu.VMEM) for a in args
    ]
    return pl.pallas_call(
        body,
        out_shape=shapes,
        in_specs=specs,
        out_specs=[pl.BlockSpec(memory_space=pltpu.VMEM) for _ in shapes],
        compiler_params=pltpu.CompilerParams(vmem_limit_bytes=min(2 * moved + (6 << 20), 40 << 20) if body is not pack_body else None),
        cost_estimate=pl.CostEstimate(flops=flops, bytes_accessed=moved, transcendentals=0),
    )(*args)


def unit(tokens):
    width = tokens.shape[1]
    centered = tokens - jnp.sum(tokens, axis=1, keepdims=True) / width
    inv_scale = lax.rsqrt(jnp.sum(centered * centered, axis=1, keepdims=True) / width + epsilon)
    return centered * inv_scale, inv_scale


def pack_body(tokens, cotangent, w_in, w_out, out, block):
    hidden = w_in.shape[1]
    block[0] = w_in[...]
    block[1, :hidden] = w_out[:, :hidden]
    block[1, hidden:] = w_out[:, hidden:]
    features = out.shape[2]
    normed = unit(tokens[...].astype(f32))[0]
    grads = cotangent[...].astype(f32)
    for part in range(ZH):
        cut = slice(part * features, (part + 1) * features)
        pair = jnp.concatenate([normed[:, cut], grads[:, cut]], axis=0).astype(bf16)
        out[part * ZL : (part + 1) * ZL] = jnp.broadcast_to(pair[None], (ZL,) + pair.shape)


def place(here, step, width):
    return pl.multiple_of(lax.rem(here + step, Y) * width, 128)


def line_up(rows, other, index, cut):
    return jnp.concatenate([ref[at, index, :, cut] for ref in (rows, other) for at in range(X)], axis=0)


def hidden_body(here, rows, other, b0, b1, b3, far_in, far_out, out):
    width, hidden = far_in.shape
    pre = grad = None
    for step, (ins, cols) in enumerate(
        ((b0.at[0], b0.at[1]), (b1.at[0], b1.at[1]), (far_in, far_out), (b3.at[0], b3.at[1]))
    ):
        at = place(here[0], step, width)
        left = line_up(rows, other, 0, pl.ds(at, width))
        terms = [dot(left, ins[...])]
        for part in range(width // hidden):
            cut = pl.ds(pl.multiple_of(at + part * hidden, 128), hidden)
            right = line_up(rows, other, 1, cut)
            terms.append(dot(right, cols[part * hidden : (part + 1) * hidden], LAST))
        one, two = terms[0], sum(terms[1:])
        pre = one if pre is None else pre + one
        grad = two if grad is None else grad + two
    out[0] = pre.astype(bf16)
    out[1] = grad.astype(bf16)


def split_body(rows, out):
    width = out.shape[3]
    for step in range(Y):
        for index in range(2):
            cut = slice(step * width, (step + 1) * width)
            out[step, index] = jnp.concatenate([rows[at, index, :, cut] for at in range(X)], axis=0)


def output_body(here, parts, b0, b1, b3, far_in, far_out, pair, keep, give):
    width, hidden = far_in.shape
    half = keep.shape[1]
    value = parts[0, 0].astype(f32) + parts[1, 0].astype(f32)
    upstream = parts[0, 1].astype(f32) + parts[1, 1].astype(f32)
    square = value * value
    curve = jnp.tanh(RATE * (value + CUBE * (square * value)))
    chance = 0.5 * (1.0 + curve)
    slope = chance + 0.5 * value * (1.0 - curve * curve) * (RATE * (1.0 + 3.0 * CUBE * square))
    act = (value * chance).astype(bf16)
    pre_grad = (upstream * slope).astype(bf16)
    pair[0] = act
    pair[1] = pre_grad
    for step, (ins, cols) in enumerate(
        ((b0.at[0], b0.at[1]), (b1.at[0], b1.at[1]), (far_in, far_out), (b3.at[0], b3.at[1]))
    ):
        at = place(here[0], step, width)
        term = dot(pre_grad, ins[...], LAST)
        keep[1, :, pl.ds(at, width)] = term[:half]
        give[1, :, pl.ds(at, width)] = term[half:].astype(bf16)
        for part in range(width // hidden):
            cut = pl.ds(pl.multiple_of(at + part * hidden, 128), hidden)
            term = dot(act, cols[part * hidden : (part + 1) * hidden])
            keep[0, :, cut] = term[:half]
            give[0, :, cut] = term[half:].astype(bf16)


def weight_body(full, mine, theirs, grad_w_in, grad_w_out):
    count = mine.shape[2]
    ins = outs = None
    for step in range(Y * CORE):
        at = slice(step * count, (step + 1) * count)
        rows = (mine, theirs)[step % CORE].at[step // CORE]
        one, two = dot(rows[0], full[1, at], FIRST), dot(full[0, at], rows[1], FIRST)
        ins = one if ins is None else ins + one
        outs = two if outs is None else outs + two
    grad_w_in[...] = ins
    grad_w_out[...] = outs


def add_body(keep, far, out):
    rows = out.shape[2]
    for step in range(X):
        at = slice(step * rows, (step + 1) * rows)
        out[step] = (keep[:, at] + far[:, at].astype(f32)).astype(bf16)


def sum_body(parts, out):
    first, second = (
        sum(parts[step, index].astype(f32) for step in range(X)).astype(bf16).astype(f32) for index in range(2)
    )
    for row in range(out.shape[0]):
        cut = slice(row, row + 1)
        out[row] = jnp.concatenate([first[cut], second[cut]], axis=0).astype(bf16)


def final_body(tokens, cotangent, sums, mixed, grad_tokens):
    features = sums.shape[2]
    tokens_wide = tokens[...].astype(f32)
    unit_rows, inv_scale = unit(tokens_wide)
    halves = [
        jnp.sum(sums[part * ZL : (part + 1) * ZL].astype(f32), axis=0) for part in range(ZH)
    ]
    whole = jnp.concatenate(halves, axis=1)
    count = ZH * features
    mixed[...] = (tokens_wide + whole[0:1]).astype(bf16)
    normed_grad = whole[1:2]
    inner = jnp.sum(normed_grad * unit_rows, axis=1, keepdims=True) / count
    mean = jnp.sum(normed_grad, axis=1, keepdims=True) / count
    through = inv_scale * (normed_grad - mean - unit_rows * inner)
    grad_tokens[...] = (cotangent[...].astype(f32) + through).astype(bf16)


def local(tokens, w_in, w_out, cotangent):
    width, hidden = w_in.shape
    features = Y * width
    count = X * ZL * ZH * CORE
    half = count // CORE
    here = lax.axis_index("y").reshape(1).astype(jnp.int32)
    shape = jax.ShapeDtypeStruct
    work = 4 * count * features * hidden

    both, block = call(
        pack_body,
        [shape((ZH * ZL, 2, features), bf16), shape((2, width, hidden), bf16)],
        tokens, cotangent, w_in, w_out,
    )
    both, block = lax.optimization_barrier((both, block))
    below, above = shift(block, "y", 1), shift(block, "y", -1)
    both = trade(both, FAR).transpose(1, 0, 2)
    rows = trade(jnp.broadcast_to(both, (X,) + both.shape), "x")
    far_in, far_out = shift(below[0], "y", 1), shift(above[1], "y", -1)
    (mine,) = call(split_body, [shape((Y, 2, half, width), bf16)], rows)
    rows, far_in, far_out, mine = lax.optimization_barrier((rows, far_in, far_out, mine))
    other = swap(rows, "core")
    mine = trade(mine, "y")
    blocks = (block, above, below, far_in, far_out)

    (parts,) = call(hidden_body, [shape((2, count, hidden), bf16)], here, rows, other, *blocks, flops=work)
    parts, mine = lax.optimization_barrier((lax.all_gather(parts, "zh"), mine))
    pair, keep, give = call(
        output_body,
        [shape((2, count, hidden), bf16), shape((2, half, features), f32), shape((2, half, features), bf16)],
        here, parts, *blocks, flops=work,
    )

    (sums,) = call(add_body, [shape((X, 2, half // X, features), bf16)], keep, swap(give, "core"))
    sums, pair, mine = lax.optimization_barrier((sums, pair, mine))
    full = lax.all_gather(pair, "y", axis=1, tiled=True)
    sums, full, theirs = lax.optimization_barrier((trade(sums, "x"), full, swap(mine, "core")))
    (sums,) = call(sum_body, [shape((half // X, 2, features), bf16)], sums)
    sums = trade(sums, FAR)

    grad_w_in, grad_w_out = call(
        weight_body,
        [shape((width, hidden), f32), shape((hidden, width), f32)],
        full, mine, theirs, flops=work,
    )

    sums, grad_w_in, grad_w_out = lax.optimization_barrier((sums, grad_w_in, grad_w_out))
    mixed, grad_tokens = call(
        final_body, [shape(tokens.shape, bf16)] * 2, tokens, cotangent, sums
    )
    return (mixed, grad_tokens, grad_w_in, grad_w_out)


def solution(mesh):
    fine = Mesh(mesh.devices.reshape(SIZES), AXES)
    dp, mp = ("zh", "y"), ("zl", "x", "core")
    return jax.shard_map(
        local,
        mesh=fine,
        in_specs=(P(dp + mp, None), P(dp, mp), P(mp, dp), P(dp + mp, None)),
        out_specs=(P(dp + mp, None), P(dp + mp, None), P(dp, mp), P(mp, dp)),
        check_vma=False,
    )
```

```python
import jax
import jax.numpy as jnp
from jax import lax
from jax.experimental import pallas as pl
from jax.experimental.pallas import tpu as pltpu
from jax.sharding import Mesh, PartitionSpec as P

epsilon = 1e-06
AXES = ("zh", "y", "zl", "x", "core")
SIZES = (2, 4, 8, 4, 2)
ZH, Y, ZL, X, CORE = SIZES
FAR = ("zh", "zl")
f32 = jnp.float32
bf16 = jnp.bfloat16
LAST = (((1,), (1,)), ((), ()))
FIRST = (((0,), (0,)), ((), ()))
RATE = 0.7978845608028654
CUBE = 0.044715


def swap(values, axis):
    return lax.ppermute(values, axis, [(0, 1), (1, 0)])


def shift(values, axis, step):
    count = lax.axis_size(axis)
    return lax.ppermute(values, axis, [(at, (at + step) % count) for at in range(count)])


def trade(values, axis):
    return lax.all_to_all(values, axis, split_axis=0, concat_axis=0, tiled=True)


def dot(left, right, contract=(((1,), (0,)), ((), ()))):
    return lax.dot_general(left, right, contract, preferred_element_type=f32)


def call(body, shapes, *args, flops=0):
    moved = sum(a.size * a.dtype.itemsize for a in args) + sum(s.size * s.dtype.itemsize for s in shapes)
    specs = [
        pl.BlockSpec(memory_space=pltpu.SMEM if a.dtype == jnp.int32 else pltpu.VMEM) for a in args
    ]
    return pl.pallas_call(
        body,
        out_shape=shapes,
        in_specs=specs,
        out_specs=[pl.BlockSpec(memory_space=pltpu.VMEM) for _ in shapes],
        compiler_params=pltpu.CompilerParams(vmem_limit_bytes=min(2 * moved + (6 << 20), 40 << 20) if body is not pack_body else None),
        cost_estimate=pl.CostEstimate(flops=flops, bytes_accessed=moved, transcendentals=0),
    )(*args)


def unit(tokens):
    width = tokens.shape[1]
    centered = tokens - jnp.sum(tokens, axis=1, keepdims=True) / width
    inv_scale = lax.rsqrt(jnp.sum(centered * centered, axis=1, keepdims=True) / width + epsilon)
    return centered * inv_scale, inv_scale


def pack_body(tokens, cotangent, w_in, w_out, out, block):
    hidden = w_in.shape[1]
    block[0] = w_in[...]
    block[1, :hidden] = w_out[:, :hidden]
    block[1, hidden:] = w_out[:, hidden:]
    features = out.shape[2]
    normed = unit(tokens[...].astype(f32))[0]
    grads = cotangent[...].astype(f32)
    for part in range(ZH):
        cut = slice(part * features, (part + 1) * features)
        pair = jnp.concatenate([normed[:, cut], grads[:, cut]], axis=0).astype(bf16)
        out[part * ZL : (part + 1) * ZL] = jnp.broadcast_to(pair[None], (ZL,) + pair.shape)


def place(here, step, width):
    return pl.multiple_of(lax.rem(here + step, Y) * width, 128)


def line_up(rows, other, index, cut):
    return jnp.concatenate([ref[at, index, :, cut] for ref in (rows, other) for at in range(X)], axis=0)


def hidden_body(here, rows, other, b0, b1, b3, far_in, far_out, out):
    width, hidden = far_in.shape
    pre = grad = None
    for step, (ins, cols) in enumerate(
        ((b0.at[0], b0.at[1]), (b1.at[0], b1.at[1]), (far_in, far_out), (b3.at[0], b3.at[1]))
    ):
        at = place(here[0], step, width)
        left = line_up(rows, other, 0, pl.ds(at, width))
        terms = [dot(left, ins[...])]
        for part in range(width // hidden):
            cut = pl.ds(pl.multiple_of(at + part * hidden, 128), hidden)
            right = line_up(rows, other, 1, cut)
            terms.append(dot(right, cols[part * hidden : (part + 1) * hidden], LAST))
        one, two = terms[0], sum(terms[1:])
        pre = one if pre is None else pre + one
        grad = two if grad is None else grad + two
    out[0] = pre.astype(bf16)
    out[1] = grad.astype(bf16)


def split_body(rows, out):
    width = out.shape[3]
    for step in range(Y):
        for index in range(2):
            cut = slice(step * width, (step + 1) * width)
            out[step, index] = jnp.concatenate([rows[at, index, :, cut] for at in range(X)], axis=0)


def output_body(here, parts, b0, b1, b3, far_in, far_out, pair, keep, give):
    width, hidden = far_in.shape
    half = keep.shape[1]
    value = parts[0, 0].astype(f32) + parts[1, 0].astype(f32)
    upstream = parts[0, 1].astype(f32) + parts[1, 1].astype(f32)
    square = value * value
    curve = jnp.tanh(RATE * (value + CUBE * (square * value)))
    chance = 0.5 * (1.0 + curve)
    slope = chance + 0.5 * value * (1.0 - curve * curve) * (RATE * (1.0 + 3.0 * CUBE * square))
    act = (value * chance).astype(bf16)
    pre_grad = (upstream * slope).astype(bf16)
    pair[0] = act
    pair[1] = pre_grad
    for step, (ins, cols) in enumerate(
        ((b0.at[0], b0.at[1]), (b1.at[0], b1.at[1]), (far_in, far_out), (b3.at[0], b3.at[1]))
    ):
        at = place(here[0], step, width)
        term = dot(pre_grad, ins[...], LAST)
        keep[1, :, pl.ds(at, width)] = term[:half]
        give[1, :, pl.ds(at, width)] = term[half:].astype(bf16)
        for part in range(width // hidden):
            cut = pl.ds(pl.multiple_of(at + part * hidden, 128), hidden)
            term = dot(act, cols[part * hidden : (part + 1) * hidden])
            keep[0, :, cut] = term[:half]
            give[0, :, cut] = term[half:].astype(bf16)


def weight_body(full, mine, first, second, grad_w_in, grad_w_out):
    def every(index):
        blocks = [ref.at[step] for ref in (first, second) for step in range(Y // 2)]
        return jnp.concatenate(
            [ref[index] for step in range(Y) for ref in (mine.at[step], blocks[step])], axis=0
        )

    grad_w_in[...] = dot(every(0), full[1], FIRST)
    grad_w_out[...] = dot(full[0], every(1), FIRST)


def add_body(keep, far, out):
    rows = out.shape[2]
    for step in range(X):
        at = slice(step * rows, (step + 1) * rows)
        out[step] = (keep[:, at] + far[:, at].astype(f32)).astype(bf16)


def sum_body(parts, out):
    first, second = (
        sum(parts[step, index].astype(f32) for step in range(X)).astype(bf16).astype(f32) for index in range(2)
    )
    for row in range(out.shape[0]):
        cut = slice(row, row + 1)
        out[row] = jnp.concatenate([first[cut], second[cut]], axis=0).astype(bf16)


def final_body(tokens, cotangent, sums, mixed, grad_tokens):
    features = sums.shape[2]
    tokens_wide = tokens[...].astype(f32)
    unit_rows, inv_scale = unit(tokens_wide)
    halves = [
        jnp.sum(sums[part * ZL : (part + 1) * ZL].astype(f32), axis=0) for part in range(ZH)
    ]
    whole = jnp.concatenate(halves, axis=1)
    count = ZH * features
    mixed[...] = (tokens_wide + whole[0:1]).astype(bf16)
    normed_grad = whole[1:2]
    inner = jnp.sum(normed_grad * unit_rows, axis=1, keepdims=True) / count
    mean = jnp.sum(normed_grad, axis=1, keepdims=True) / count
    through = inv_scale * (normed_grad - mean - unit_rows * inner)
    grad_tokens[...] = (cotangent[...].astype(f32) + through).astype(bf16)


def local(tokens, w_in, w_out, cotangent):
    width, hidden = w_in.shape
    features = Y * width
    count = X * ZL * ZH * CORE
    half = count // CORE
    here = lax.axis_index("y").reshape(1).astype(jnp.int32)
    shape = jax.ShapeDtypeStruct
    work = 4 * count * features * hidden

    both, block = call(
        pack_body,
        [shape((ZH * ZL, 2, features), bf16), shape((2, width, hidden), bf16)],
        tokens, cotangent, w_in, w_out,
    )
    both, block = lax.optimization_barrier((both, block))
    below, above = shift(block, "y", 1), shift(block, "y", -1)
    both = trade(both, FAR).transpose(1, 0, 2)
    rows = trade(jnp.broadcast_to(both, (X,) + both.shape), "x")
    far_in, far_out = shift(below[0], "y", 1), shift(above[1], "y", -1)
    (mine,) = call(split_body, [shape((Y, 2, half, width), bf16)], rows)
    rows, far_in, far_out, mine = lax.optimization_barrier((rows, far_in, far_out, mine))
    other = swap(rows, "core")
    mine = trade(mine, "y")
    blocks = (block, above, below, far_in, far_out)

    (parts,) = call(hidden_body, [shape((2, count, hidden), bf16)], here, rows, other, *blocks, flops=work)
    parts, mine = lax.optimization_barrier((lax.all_gather(parts, "zh"), mine))
    pair, keep, give = call(
        output_body,
        [shape((2, count, hidden), bf16), shape((2, half, features), f32), shape((2, half, features), bf16)],
        here, parts, *blocks, flops=work,
    )

    (sums,) = call(add_body, [shape((X, 2, half // X, features), bf16)], keep, swap(give, "core"))
    sums, pair = lax.optimization_barrier((sums, pair))
    full = lax.all_gather(pair, "y", axis=1, tiled=True)
    sums, full = lax.optimization_barrier((trade(sums, "x"), full))
    (sums,) = call(sum_body, [shape((half // X, 2, features), bf16)], sums)
    sums, *pieces = lax.optimization_barrier((sums, mine[: Y // 2], mine[Y // 2 :]))
    sums = trade(sums, FAR)
    theirs = [swap(piece, "core") for piece in pieces]

    grad_w_in, grad_w_out = call(
        weight_body,
        [shape((width, hidden), f32), shape((hidden, width), f32)],
        full, mine, *theirs, flops=work,
    )

    sums, grad_w_in, grad_w_out = lax.optimization_barrier((sums, grad_w_in, grad_w_out))
    mixed, grad_tokens = call(
        final_body, [shape(tokens.shape, bf16)] * 2, tokens, cotangent, sums
    )
    return (mixed, grad_tokens, grad_w_in, grad_w_out)


def solution(mesh):
    fine = Mesh(mesh.devices.reshape(SIZES), AXES)
    dp, mp = ("zh", "y"), ("zl", "x", "core")
    return jax.shard_map(
        local,
        mesh=fine,
        in_specs=(P(dp + mp, None), P(dp, mp), P(mp, dp), P(dp + mp, None)),
        out_specs=(P(dp + mp, None), P(dp + mp, None), P(dp, mp), P(mp, dp)),
        check_vma=False,
    )
```

```python
import jax
import jax.numpy as jnp
from jax import lax
from jax.experimental import pallas as pl
from jax.experimental.pallas import tpu as pltpu
from jax.sharding import Mesh, PartitionSpec as P

epsilon = 1e-06
AXES = ("zh", "y", "zl", "x", "core")
SIZES = (2, 4, 8, 4, 2)
ZH, Y, ZL, X, CORE = SIZES
FAR = ("zh", "zl")
f32 = jnp.float32
bf16 = jnp.bfloat16
LAST = (((1,), (1,)), ((), ()))
FIRST = (((0,), (0,)), ((), ()))
RATE = 0.7978845608028654
CUBE = 0.044715


def swap(values, axis):
    return lax.ppermute(values, axis, [(0, 1), (1, 0)])


def shift(values, axis, step):
    count = lax.axis_size(axis)
    return lax.ppermute(values, axis, [(at, (at + step) % count) for at in range(count)])


def trade(values, axis):
    return lax.all_to_all(values, axis, split_axis=0, concat_axis=0, tiled=True)


def dot(left, right, contract=(((1,), (0,)), ((), ()))):
    return lax.dot_general(left, right, contract, preferred_element_type=f32)


def call(body, shapes, *args, flops=0):
    moved = sum(a.size * a.dtype.itemsize for a in args) + sum(s.size * s.dtype.itemsize for s in shapes)
    specs = [
        pl.BlockSpec(memory_space=pltpu.SMEM if a.dtype == jnp.int32 else pltpu.VMEM) for a in args
    ]
    return pl.pallas_call(
        body,
        out_shape=shapes,
        in_specs=specs,
        out_specs=[pl.BlockSpec(memory_space=pltpu.VMEM) for _ in shapes],
        compiler_params=pltpu.CompilerParams(vmem_limit_bytes=min(2 * moved + (6 << 20), 40 << 20) if body is not pack_body else None),
        cost_estimate=pl.CostEstimate(flops=flops, bytes_accessed=moved, transcendentals=0),
    )(*args)


def unit(tokens):
    width = tokens.shape[1]
    centered = tokens - jnp.sum(tokens, axis=1, keepdims=True) / width
    inv_scale = lax.rsqrt(jnp.sum(centered * centered, axis=1, keepdims=True) / width + epsilon)
    return centered * inv_scale, inv_scale


def pack_body(tokens, cotangent, w_in, w_out, out, block):
    hidden = w_in.shape[1]
    block[0] = w_in[...]
    block[1, :hidden] = w_out[:, :hidden]
    block[1, hidden:] = w_out[:, hidden:]
    features = out.shape[2]
    normed = unit(tokens[...].astype(f32))[0]
    grads = cotangent[...].astype(f32)
    for part in range(ZH):
        cut = slice(part * features, (part + 1) * features)
        pair = jnp.concatenate([normed[:, cut], grads[:, cut]], axis=0).astype(bf16)
        out[part * ZL : (part + 1) * ZL] = jnp.broadcast_to(pair[None], (ZL,) + pair.shape)


def place(here, step, width):
    return pl.multiple_of(lax.rem(here + step, Y) * width, 128)


def line_up(rows, other, index, cut):
    return jnp.concatenate([ref[at, index, :, cut] for ref in (rows, other) for at in range(X)], axis=0)


def hidden_body(here, rows, other, b0, b1, b3, far_in, far_out, out):
    width, hidden = far_in.shape
    pre = grad = None
    for step, (ins, cols) in enumerate(
        ((b0.at[0], b0.at[1]), (b1.at[0], b1.at[1]), (far_in, far_out), (b3.at[0], b3.at[1]))
    ):
        at = place(here[0], step, width)
        left = line_up(rows, other, 0, pl.ds(at, width))
        terms = [dot(left, ins[...])]
        for part in range(width // hidden):
            cut = pl.ds(pl.multiple_of(at + part * hidden, 128), hidden)
            right = line_up(rows, other, 1, cut)
            terms.append(dot(right, cols[part * hidden : (part + 1) * hidden], LAST))
        one, two = terms[0], sum(terms[1:])
        pre = one if pre is None else pre + one
        grad = two if grad is None else grad + two
    out[0] = pre.astype(bf16)
    out[1] = grad.astype(bf16)


def split_body(rows, out):
    width = out.shape[3]
    for step in range(Y):
        for index in range(2):
            cut = slice(step * width, (step + 1) * width)
            out[step, index] = jnp.concatenate([rows[at, index, :, cut] for at in range(X)], axis=0)


def output_body(here, parts, b0, b1, b3, far_in, far_out, pair, keep, give):
    width, hidden = far_in.shape
    half = keep.shape[1]
    value = parts[0, 0].astype(f32) + parts[1, 0].astype(f32)
    upstream = parts[0, 1].astype(f32) + parts[1, 1].astype(f32)
    square = value * value
    curve = jnp.tanh(RATE * (value + CUBE * (square * value)))
    chance = 0.5 * (1.0 + curve)
    slope = chance + 0.5 * value * (1.0 - curve * curve) * (RATE * (1.0 + 3.0 * CUBE * square))
    act = (value * chance).astype(bf16)
    pre_grad = (upstream * slope).astype(bf16)
    pair[0] = act
    pair[1] = pre_grad
    for step, (ins, cols) in enumerate(
        ((b0.at[0], b0.at[1]), (b1.at[0], b1.at[1]), (far_in, far_out), (b3.at[0], b3.at[1]))
    ):
        at = place(here[0], step, width)
        term = dot(pre_grad, ins[...], LAST)
        keep[1, :, pl.ds(at, width)] = term[:half]
        give[1, :, pl.ds(at, width)] = term[half:].astype(bf16)
        for part in range(width // hidden):
            cut = pl.ds(pl.multiple_of(at + part * hidden, 128), hidden)
            term = dot(act, cols[part * hidden : (part + 1) * hidden])
            keep[0, :, cut] = term[:half]
            give[0, :, cut] = term[half:].astype(bf16)


def weight_body(full, mine, first, second, grad_w_in, grad_w_out):
    def every(index):
        blocks = [ref.at[step] for ref in (first, second) for step in range(Y // 2)]
        return jnp.concatenate(
            [ref[index] for step in range(Y) for ref in (mine.at[step], blocks[step])], axis=0
        )

    grad_w_in[...] = dot(every(0), full[1], FIRST)
    grad_w_out[...] = dot(full[0], every(1), FIRST)


def add_body(keep, far, out):
    rows = out.shape[2]
    for step in range(X):
        at = slice(step * rows, (step + 1) * rows)
        out[step] = (keep[:, at] + far[:, at].astype(f32)).astype(bf16)


def sum_body(parts, out):
    first, second = (
        sum(parts[step, index].astype(f32) for step in range(X)).astype(bf16).astype(f32) for index in range(2)
    )
    for row in range(out.shape[0]):
        cut = slice(row, row + 1)
        out[row] = jnp.concatenate([first[cut], second[cut]], axis=0).astype(bf16)


def final_body(tokens, cotangent, sums, mixed, grad_tokens):
    features = sums.shape[2]
    tokens_wide = tokens[...].astype(f32)
    unit_rows, inv_scale = unit(tokens_wide)
    halves = [
        jnp.sum(sums[part * ZL : (part + 1) * ZL].astype(f32), axis=0) for part in range(ZH)
    ]
    whole = jnp.concatenate(halves, axis=1)
    count = ZH * features
    mixed[...] = (tokens_wide + whole[0:1]).astype(bf16)
    normed_grad = whole[1:2]
    inner = jnp.sum(normed_grad * unit_rows, axis=1, keepdims=True) / count
    mean = jnp.sum(normed_grad, axis=1, keepdims=True) / count
    through = inv_scale * (normed_grad - mean - unit_rows * inner)
    grad_tokens[...] = (cotangent[...].astype(f32) + through).astype(bf16)


def local(tokens, w_in, w_out, cotangent):
    width, hidden = w_in.shape
    features = Y * width
    count = X * ZL * ZH * CORE
    half = count // CORE
    here = lax.axis_index("y").reshape(1).astype(jnp.int32)
    shape = jax.ShapeDtypeStruct
    work = 4 * count * features * hidden

    both, block = call(
        pack_body,
        [shape((ZH * ZL, 2, features), bf16), shape((2, width, hidden), bf16)],
        tokens, cotangent, w_in, w_out,
    )
    both, block = lax.optimization_barrier((both, block))
    below, above = shift(block, "y", 1), shift(block, "y", -1)
    both = trade(both, FAR).transpose(1, 0, 2)
    rows = trade(jnp.broadcast_to(both, (X,) + both.shape), "x")
    far_in, far_out = shift(below[0], "y", 1), shift(above[1], "y", -1)
    (mine,) = call(split_body, [shape((Y, 2, half, width), bf16)], rows)
    other = swap(rows, "core")
    mine = trade(mine, "y")
    rows, far_in, far_out = lax.optimization_barrier((rows, far_in, far_out))
    blocks = (block, above, below, far_in, far_out)

    (parts,) = call(hidden_body, [shape((2, count, hidden), bf16)], here, rows, other, *blocks, flops=work)
    parts, mine = lax.optimization_barrier((lax.all_gather(parts, "zh"), mine))
    pair, keep, give = call(
        output_body,
        [shape((2, count, hidden), bf16), shape((2, half, features), f32), shape((2, half, features), bf16)],
        here, parts, *blocks, flops=work,
    )

    (sums,) = call(add_body, [shape((X, 2, half // X, features), bf16)], keep, swap(give, "core"))
    sums, pair = lax.optimization_barrier((sums, pair))
    full = lax.all_gather(pair, "y", axis=1, tiled=True)
    sums, full = lax.optimization_barrier((trade(sums, "x"), full))
    (sums,) = call(sum_body, [shape((half // X, 2, features), bf16)], sums)
    sums, *pieces = lax.optimization_barrier((sums, mine[: Y // 2], mine[Y // 2 :]))
    sums = trade(sums, FAR)
    theirs = [swap(piece, "core") for piece in pieces]

    grad_w_in, grad_w_out = call(
        weight_body,
        [shape((width, hidden), f32), shape((hidden, width), f32)],
        full, mine, *theirs, flops=work,
    )

    sums, grad_w_in, grad_w_out = lax.optimization_barrier((sums, grad_w_in, grad_w_out))
    mixed, grad_tokens = call(
        final_body, [shape(tokens.shape, bf16)] * 2, tokens, cotangent, sums
    )
    return (mixed, grad_tokens, grad_w_in, grad_w_out)


def solution(mesh):
    fine = Mesh(mesh.devices.reshape(SIZES), AXES)
    dp, mp = ("zh", "y"), ("zl", "x", "core")
    return jax.shard_map(
        local,
        mesh=fine,
        in_specs=(P(dp + mp, None), P(dp, mp), P(mp, dp), P(dp + mp, None)),
        out_specs=(P(dp + mp, None), P(dp + mp, None), P(dp, mp), P(mp, dp)),
        check_vma=False,
    )
```

```python
import jax
import jax.numpy as jnp
from jax import lax
from jax.experimental import pallas as pl
from jax.experimental.pallas import tpu as pltpu
from jax.sharding import Mesh, PartitionSpec as P

epsilon = 1e-06
AXES = ("zh", "y", "zl", "x", "core")
SIZES = (2, 4, 8, 4, 2)
ZH, Y, ZL, X, CORE = SIZES
FAR = ("zh", "zl")
f32 = jnp.float32
bf16 = jnp.bfloat16
LAST = (((1,), (1,)), ((), ()))
FIRST = (((0,), (0,)), ((), ()))
RATE = 0.7978845608028654
CUBE = 0.044715


def swap(values, axis):
    return lax.ppermute(values, axis, [(0, 1), (1, 0)])


def shift(values, axis, step):
    count = lax.axis_size(axis)
    return lax.ppermute(values, axis, [(at, (at + step) % count) for at in range(count)])


def trade(values, axis):
    return lax.all_to_all(values, axis, split_axis=0, concat_axis=0, tiled=True)


def dot(left, right, contract=(((1,), (0,)), ((), ()))):
    return lax.dot_general(left, right, contract, preferred_element_type=f32)


def call(body, shapes, *args, flops=0):
    moved = sum(a.size * a.dtype.itemsize for a in args) + sum(s.size * s.dtype.itemsize for s in shapes)
    specs = [
        pl.BlockSpec(memory_space=pltpu.SMEM if a.dtype == jnp.int32 else pltpu.VMEM) for a in args
    ]
    return pl.pallas_call(
        body,
        out_shape=shapes,
        in_specs=specs,
        out_specs=[pl.BlockSpec(memory_space=pltpu.VMEM) for _ in shapes],
        compiler_params=pltpu.CompilerParams(vmem_limit_bytes=min(2 * moved + (6 << 20), 40 << 20) if body is not pack_body else None),
        cost_estimate=pl.CostEstimate(flops=flops, bytes_accessed=moved, transcendentals=0),
    )(*args)


def unit(tokens):
    width = tokens.shape[1]
    centered = tokens - jnp.sum(tokens, axis=1, keepdims=True) / width
    inv_scale = lax.rsqrt(jnp.sum(centered * centered, axis=1, keepdims=True) / width + epsilon)
    return centered * inv_scale, inv_scale


def pack_body(tokens, cotangent, w_in, w_out, out, block):
    hidden = w_in.shape[1]
    block[0] = w_in[...]
    block[1, :hidden] = w_out[:, :hidden]
    block[1, hidden:] = w_out[:, hidden:]
    features = out.shape[2]
    normed = unit(tokens[...].astype(f32))[0]
    grads = cotangent[...].astype(f32)
    for part in range(ZH):
        cut = slice(part * features, (part + 1) * features)
        pair = jnp.concatenate([normed[:, cut], grads[:, cut]], axis=0).astype(bf16)
        out[part * ZL : (part + 1) * ZL] = jnp.broadcast_to(pair[None], (ZL,) + pair.shape)


def place(here, step, width):
    return pl.multiple_of(lax.rem(here + step, Y) * width, 128)


def line_up(rows, other, index, cut):
    return jnp.concatenate([ref[at, index, :, cut] for ref in (rows, other) for at in range(X)], axis=0)


def hidden_body(here, rows, other, b0, b1, b3, far_in, far_out, out):
    width, hidden = far_in.shape
    pre = grad = None
    for step, (ins, cols) in enumerate(
        ((b0.at[0], b0.at[1]), (b1.at[0], b1.at[1]), (far_in, far_out), (b3.at[0], b3.at[1]))
    ):
        at = place(here[0], step, width)
        left = line_up(rows, other, 0, pl.ds(at, width))
        terms = [dot(left, ins[...])]
        for part in range(width // hidden):
            cut = pl.ds(pl.multiple_of(at + part * hidden, 128), hidden)
            right = line_up(rows, other, 1, cut)
            terms.append(dot(right, cols[part * hidden : (part + 1) * hidden], LAST))
        one, two = terms[0], sum(terms[1:])
        pre = one if pre is None else pre + one
        grad = two if grad is None else grad + two
    out[0] = pre.astype(bf16)
    out[1] = grad.astype(bf16)


def split_body(rows, out):
    width = out.shape[3]
    for step in range(Y):
        for index in range(2):
            cut = slice(step * width, (step + 1) * width)
            out[step, index] = jnp.concatenate([rows[at, index, :, cut] for at in range(X)], axis=0)


def output_body(here, parts, b0, b1, b3, far_in, far_out, pair, keep, give):
    width, hidden = far_in.shape
    half = keep.shape[1]
    value = parts[0, 0].astype(f32) + parts[1, 0].astype(f32)
    upstream = parts[0, 1].astype(f32) + parts[1, 1].astype(f32)
    square = value * value
    curve = jnp.tanh(RATE * (value + CUBE * (square * value)))
    chance = 0.5 * (1.0 + curve)
    slope = chance + 0.5 * value * (1.0 - curve * curve) * (RATE * (1.0 + 3.0 * CUBE * square))
    act = (value * chance).astype(bf16)
    pre_grad = (upstream * slope).astype(bf16)
    pair[0] = act
    pair[1] = pre_grad
    for step, (ins, cols) in enumerate(
        ((b0.at[0], b0.at[1]), (b1.at[0], b1.at[1]), (far_in, far_out), (b3.at[0], b3.at[1]))
    ):
        at = place(here[0], step, width)
        term = dot(pre_grad, ins[...], LAST)
        keep[1, :, pl.ds(at, width)] = term[:half]
        give[1, :, pl.ds(at, width)] = term[half:].astype(bf16)
        for part in range(width // hidden):
            cut = pl.ds(pl.multiple_of(at + part * hidden, 128), hidden)
            term = dot(act, cols[part * hidden : (part + 1) * hidden])
            keep[0, :, cut] = term[:half]
            give[0, :, cut] = term[half:].astype(bf16)


def weight_body(full, mine, first, second, grad_w_in, grad_w_out):
    def every(index):
        blocks = [ref.at[step] for ref in (first, second) for step in range(Y // 2)]
        return jnp.concatenate(
            [ref[index] for step in range(Y) for ref in (mine.at[step], blocks[step])], axis=0
        )

    grad_w_in[...] = dot(every(0), full[1], FIRST)
    grad_w_out[...] = dot(full[0], every(1), FIRST)


def add_body(keep, far, out):
    rows = out.shape[2]
    for step in range(X):
        at = slice(step * rows, (step + 1) * rows)
        out[step] = (keep[:, at] + far[:, at].astype(f32)).astype(bf16)


def sum_body(parts, out):
    first, second = (
        sum(parts[step, index].astype(f32) for step in range(X)).astype(bf16).astype(f32) for index in range(2)
    )
    for row in range(out.shape[0]):
        cut = slice(row, row + 1)
        out[row] = jnp.concatenate([first[cut], second[cut]], axis=0).astype(bf16)


def final_body(tokens, cotangent, sums, mixed, grad_tokens):
    features = sums.shape[2]
    tokens_wide = tokens[...].astype(f32)
    unit_rows, inv_scale = unit(tokens_wide)
    halves = [
        jnp.sum(sums[part * ZL : (part + 1) * ZL].astype(f32), axis=0) for part in range(ZH)
    ]
    whole = jnp.concatenate(halves, axis=1)
    count = ZH * features
    mixed[...] = (tokens_wide + whole[0:1]).astype(bf16)
    normed_grad = whole[1:2]
    inner = jnp.sum(normed_grad * unit_rows, axis=1, keepdims=True) / count
    mean = jnp.sum(normed_grad, axis=1, keepdims=True) / count
    through = inv_scale * (normed_grad - mean - unit_rows * inner)
    grad_tokens[...] = (cotangent[...].astype(f32) + through).astype(bf16)


def local(tokens, w_in, w_out, cotangent):
    width, hidden = w_in.shape
    features = Y * width
    count = X * ZL * ZH * CORE
    half = count // CORE
    here = lax.axis_index("y").reshape(1).astype(jnp.int32)
    shape = jax.ShapeDtypeStruct
    work = 4 * count * features * hidden

    both, block = call(
        pack_body,
        [shape((ZH * ZL, 2, features), bf16), shape((2, width, hidden), bf16)],
        tokens, cotangent, w_in, w_out,
    )
    both, block = lax.optimization_barrier((both, block))
    below, above = shift(block, "y", 1), shift(block, "y", -1)
    both = trade(both, FAR).transpose(1, 0, 2)
    rows = trade(jnp.broadcast_to(both, (X,) + both.shape), "x")
    far_in, far_out = shift(below[0], "y", 1), shift(above[1], "y", -1)
    (mine,) = call(split_body, [shape((Y, 2, half, width), bf16)], rows)
    other = swap(rows, "core")
    far_in, far_out, mine = lax.optimization_barrier((far_in, far_out, mine))
    mine = trade(mine, "y")
    blocks = (block, above, below, far_in, far_out)

    (parts,) = call(hidden_body, [shape((2, count, hidden), bf16)], here, rows, other, *blocks, flops=work)
    parts, mine = lax.optimization_barrier((lax.all_gather(parts, "zh"), mine))
    pair, keep, give = call(
        output_body,
        [shape((2, count, hidden), bf16), shape((2, half, features), f32), shape((2, half, features), bf16)],
        here, parts, *blocks, flops=work,
    )

    (sums,) = call(add_body, [shape((X, 2, half // X, features), bf16)], keep, swap(give, "core"))
    sums, pair = lax.optimization_barrier((sums, pair))
    full = lax.all_gather(pair, "y", axis=1, tiled=True)
    sums, full = lax.optimization_barrier((trade(sums, "x"), full))
    (sums,) = call(sum_body, [shape((half // X, 2, features), bf16)], sums)
    sums, mine = lax.optimization_barrier((sums, mine))
    sums = trade(sums, FAR)
    theirs = [swap(piece, "core") for piece in (mine[: Y // 2], mine[Y // 2 :])]

    grad_w_in, grad_w_out = call(
        weight_body,
        [shape((width, hidden), f32), shape((hidden, width), f32)],
        full, mine, *theirs, flops=work,
    )

    sums, grad_w_in, grad_w_out = lax.optimization_barrier((sums, grad_w_in, grad_w_out))
    mixed, grad_tokens = call(
        final_body, [shape(tokens.shape, bf16)] * 2, tokens, cotangent, sums
    )
    return (mixed, grad_tokens, grad_w_in, grad_w_out)


def solution(mesh):
    fine = Mesh(mesh.devices.reshape(SIZES), AXES)
    dp, mp = ("zh", "y"), ("zl", "x", "core")
    return jax.shard_map(
        local,
        mesh=fine,
        in_specs=(P(dp + mp, None), P(dp, mp), P(mp, dp), P(dp + mp, None)),
        out_specs=(P(dp + mp, None), P(dp + mp, None), P(dp, mp), P(mp, dp)),
        check_vma=False,
    )
```

```python
import jax
import jax.numpy as jnp
from jax import lax
from jax.experimental import pallas as pl
from jax.experimental.pallas import tpu as pltpu
from jax.sharding import Mesh, PartitionSpec as P

epsilon = 1e-06
AXES = ("zh", "y", "zl", "x", "core")
SIZES = (2, 4, 8, 4, 2)
ZH, Y, ZL, X, CORE = SIZES
FAR = ("zh", "zl")
f32 = jnp.float32
bf16 = jnp.bfloat16
LAST = (((1,), (1,)), ((), ()))
FIRST = (((0,), (0,)), ((), ()))
RATE = 0.7978845608028654
CUBE = 0.044715


def swap(values, axis):
    return lax.ppermute(values, axis, [(0, 1), (1, 0)])


def shift(values, axis, step):
    count = lax.axis_size(axis)
    return lax.ppermute(values, axis, [(at, (at + step) % count) for at in range(count)])


def trade(values, axis):
    return lax.all_to_all(values, axis, split_axis=0, concat_axis=0, tiled=True)


def dot(left, right, contract=(((1,), (0,)), ((), ()))):
    return lax.dot_general(left, right, contract, preferred_element_type=f32)


def call(body, shapes, *args, flops=0):
    moved = sum(a.size * a.dtype.itemsize for a in args) + sum(s.size * s.dtype.itemsize for s in shapes)
    specs = [
        pl.BlockSpec(memory_space=pltpu.SMEM if a.dtype == jnp.int32 else pltpu.VMEM) for a in args
    ]
    return pl.pallas_call(
        body,
        out_shape=shapes,
        in_specs=specs,
        out_specs=[pl.BlockSpec(memory_space=pltpu.VMEM) for _ in shapes],
        compiler_params=pltpu.CompilerParams(vmem_limit_bytes=min(2 * moved + (6 << 20), 40 << 20) if body is not pack_body else None),
        cost_estimate=pl.CostEstimate(flops=flops, bytes_accessed=moved, transcendentals=0),
    )(*args)


def unit(tokens):
    width = tokens.shape[1]
    centered = tokens - jnp.sum(tokens, axis=1, keepdims=True) / width
    inv_scale = lax.rsqrt(jnp.sum(centered * centered, axis=1, keepdims=True) / width + epsilon)
    return centered * inv_scale, inv_scale


def pack_body(tokens, cotangent, w_in, w_out, out, block):
    hidden = w_in.shape[1]
    block[0] = w_in[...]
    block[1, :hidden] = w_out[:, :hidden]
    block[1, hidden:] = w_out[:, hidden:]
    features = out.shape[2]
    normed = unit(tokens[...].astype(f32))[0]
    grads = cotangent[...].astype(f32)
    for part in range(ZH):
        cut = slice(part * features, (part + 1) * features)
        pair = jnp.concatenate([normed[:, cut], grads[:, cut]], axis=0).astype(bf16)
        out[part * ZL : (part + 1) * ZL] = jnp.broadcast_to(pair[None], (ZL,) + pair.shape)


def place(here, step, width):
    return pl.multiple_of(lax.rem(here + step, Y) * width, 128)


def line_up(rows, other, index, cut):
    return jnp.concatenate([ref[at, index, :, cut] for ref in (rows, other) for at in range(X)], axis=0)


def hidden_body(here, rows, other, b0, b1, b3, far_in, far_out, out):
    width, hidden = far_in.shape
    pre = grad = None
    for step, (ins, cols) in enumerate(
        ((b0.at[0], b0.at[1]), (b1.at[0], b1.at[1]), (far_in, far_out), (b3.at[0], b3.at[1]))
    ):
        at = place(here[0], step, width)
        left = line_up(rows, other, 0, pl.ds(at, width))
        terms = [dot(left, ins[...])]
        for part in range(width // hidden):
            cut = pl.ds(pl.multiple_of(at + part * hidden, 128), hidden)
            right = line_up(rows, other, 1, cut)
            terms.append(dot(right, cols[part * hidden : (part + 1) * hidden], LAST))
        one, two = terms[0], sum(terms[1:])
        pre = one if pre is None else pre + one
        grad = two if grad is None else grad + two
    out[0] = pre.astype(bf16)
    out[1] = grad.astype(bf16)


def split_body(rows, out):
    width = out.shape[3]
    for step in range(Y):
        for index in range(2):
            cut = slice(step * width, (step + 1) * width)
            out[step, index] = jnp.concatenate([rows[at, index, :, cut] for at in range(X)], axis=0)


def output_body(here, parts, b0, b1, b3, far_in, far_out, pair, keep, give):
    width, hidden = far_in.shape
    half = keep.shape[1]
    value = parts[0, 0].astype(f32) + parts[1, 0].astype(f32)
    upstream = parts[0, 1].astype(f32) + parts[1, 1].astype(f32)
    square = value * value
    curve = jnp.tanh(RATE * (value + CUBE * (square * value)))
    chance = 0.5 * (1.0 + curve)
    slope = chance + 0.5 * value * (1.0 - curve * curve) * (RATE * (1.0 + 3.0 * CUBE * square))
    act = (value * chance).astype(bf16)
    pre_grad = (upstream * slope).astype(bf16)
    pair[0] = act
    pair[1] = pre_grad
    for step, (ins, cols) in enumerate(
        ((b0.at[0], b0.at[1]), (b1.at[0], b1.at[1]), (far_in, far_out), (b3.at[0], b3.at[1]))
    ):
        at = place(here[0], step, width)
        term = dot(pre_grad, ins[...], LAST)
        keep[1, :, pl.ds(at, width)] = term[:half]
        give[1, :, pl.ds(at, width)] = term[half:].astype(bf16)
        for part in range(width // hidden):
            cut = pl.ds(pl.multiple_of(at + part * hidden, 128), hidden)
            term = dot(act, cols[part * hidden : (part + 1) * hidden])
            keep[0, :, cut] = term[:half]
            give[0, :, cut] = term[half:].astype(bf16)


def weight_body(full, mine, first, second, grad_w_in, grad_w_out):
    def every(index):
        blocks = [ref.at[step] for ref in (first, second) for step in range(Y // 2)]
        return jnp.concatenate(
            [ref[index] for step in range(Y) for ref in (mine.at[step], blocks[step])], axis=0
        )

    grad_w_in[...] = dot(every(0), full[1], FIRST)
    grad_w_out[...] = dot(full[0], every(1), FIRST)


def add_body(keep, far, out):
    rows = out.shape[2]
    for step in range(X):
        at = slice(step * rows, (step + 1) * rows)
        out[step] = (keep[:, at] + far[:, at].astype(f32)).astype(bf16)


def sum_body(parts, out):
    first, second = (
        sum(parts[step, index].astype(f32) for step in range(X)).astype(bf16).astype(f32) for index in range(2)
    )
    for row in range(out.shape[0]):
        cut = slice(row, row + 1)
        out[row] = jnp.concatenate([first[cut], second[cut]], axis=0).astype(bf16)


def final_body(tokens, cotangent, sums, mixed, grad_tokens):
    features = sums.shape[2]
    tokens_wide = tokens[...].astype(f32)
    unit_rows, inv_scale = unit(tokens_wide)
    halves = [
        jnp.sum(sums[part * ZL : (part + 1) * ZL].astype(f32), axis=0) for part in range(ZH)
    ]
    whole = jnp.concatenate(halves, axis=1)
    count = ZH * features
    mixed[...] = (tokens_wide + whole[0:1]).astype(bf16)
    normed_grad = whole[1:2]
    inner = jnp.sum(normed_grad * unit_rows, axis=1, keepdims=True) / count
    mean = jnp.sum(normed_grad, axis=1, keepdims=True) / count
    through = inv_scale * (normed_grad - mean - unit_rows * inner)
    grad_tokens[...] = (cotangent[...].astype(f32) + through).astype(bf16)


def local(tokens, w_in, w_out, cotangent):
    width, hidden = w_in.shape
    features = Y * width
    count = X * ZL * ZH * CORE
    half = count // CORE
    here = lax.axis_index("y").reshape(1).astype(jnp.int32)
    shape = jax.ShapeDtypeStruct
    work = 4 * count * features * hidden

    both, block = call(
        pack_body,
        [shape((ZH * ZL, 2, features), bf16), shape((2, width, hidden), bf16)],
        tokens, cotangent, w_in, w_out,
    )
    both, block = lax.optimization_barrier((both, block))
    below, above = shift(block, "y", 1), shift(block, "y", -1)
    both = trade(both, FAR).transpose(1, 0, 2)
    rows = trade(jnp.broadcast_to(both, (X,) + both.shape), "x")
    far_in, far_out = shift(below[0], "y", 1), shift(above[1], "y", -1)
    (mine,) = call(split_body, [shape((Y, 2, half, width), bf16)], rows)
    other = swap(rows, "core")
    far_in, far_out, mine = lax.optimization_barrier((far_in, far_out, mine))
    mine = trade(mine, "y")
    blocks = (block, above, below, far_in, far_out)

    (parts,) = call(hidden_body, [shape((2, count, hidden), bf16)], here, rows, other, *blocks, flops=work)
    parts, mine = lax.optimization_barrier((lax.all_gather(parts, "zh"), mine))
    pair, keep, give = call(
        output_body,
        [shape((2, count, hidden), bf16), shape((2, half, features), f32), shape((2, half, features), bf16)],
        here, parts, *blocks, flops=work,
    )

    (sums,) = call(add_body, [shape((X, 2, half // X, features), bf16)], keep, swap(give, "core"))
    sums, mine = lax.optimization_barrier((sums, mine))
    theirs = [swap(piece, "core") for piece in (mine[: Y // 2], mine[Y // 2 :])]
    sums, theirs = lax.optimization_barrier((trade(sums, "x"), theirs))
    (sums,) = call(sum_body, [shape((half // X, 2, features), bf16)], sums)
    sums, pair = lax.optimization_barrier((sums, pair))
    sums, full = trade(sums, FAR), lax.all_gather(pair, "y", axis=1, tiled=True)

    grad_w_in, grad_w_out = call(
        weight_body,
        [shape((width, hidden), f32), shape((hidden, width), f32)],
        full, mine, *theirs, flops=work,
    )

    sums, grad_w_in, grad_w_out = lax.optimization_barrier((sums, grad_w_in, grad_w_out))
    mixed, grad_tokens = call(
        final_body, [shape(tokens.shape, bf16)] * 2, tokens, cotangent, sums
    )
    return (mixed, grad_tokens, grad_w_in, grad_w_out)


def solution(mesh):
    fine = Mesh(mesh.devices.reshape(SIZES), AXES)
    dp, mp = ("zh", "y"), ("zl", "x", "core")
    return jax.shard_map(
        local,
        mesh=fine,
        in_specs=(P(dp + mp, None), P(dp, mp), P(mp, dp), P(dp + mp, None)),
        out_specs=(P(dp + mp, None), P(dp + mp, None), P(dp, mp), P(mp, dp)),
        check_vma=False,
    )
```

```python
import jax
import jax.numpy as jnp
from jax import lax
from jax.experimental import pallas as pl
from jax.experimental.pallas import tpu as pltpu
from jax.sharding import Mesh, PartitionSpec as P

epsilon = 1e-06
AXES = ("zh", "y", "zl", "x", "core")
SIZES = (2, 4, 8, 4, 2)
ZH, Y, ZL, X, CORE = SIZES
FAR = ("zh", "zl")
f32 = jnp.float32
bf16 = jnp.bfloat16
LAST = (((1,), (1,)), ((), ()))
FIRST = (((0,), (0,)), ((), ()))
RATE = 0.7978845608028654
CUBE = 0.044715


def swap(values, axis):
    return lax.ppermute(values, axis, [(0, 1), (1, 0)])


def shift(values, axis, step):
    count = lax.axis_size(axis)
    return lax.ppermute(values, axis, [(at, (at + step) % count) for at in range(count)])


def trade(values, axis):
    return lax.all_to_all(values, axis, split_axis=0, concat_axis=0, tiled=True)


def dot(left, right, contract=(((1,), (0,)), ((), ()))):
    return lax.dot_general(left, right, contract, preferred_element_type=f32)


def call(body, shapes, *args, flops=0):
    moved = sum(a.size * a.dtype.itemsize for a in args) + sum(s.size * s.dtype.itemsize for s in shapes)
    specs = [
        pl.BlockSpec(memory_space=pltpu.SMEM if a.dtype == jnp.int32 else pltpu.VMEM) for a in args
    ]
    return pl.pallas_call(
        body,
        out_shape=shapes,
        in_specs=specs,
        out_specs=[pl.BlockSpec(memory_space=pltpu.VMEM) for _ in shapes],
        compiler_params=pltpu.CompilerParams(vmem_limit_bytes=min(2 * moved + (6 << 20), 40 << 20) if body is not pack_body else None),
        cost_estimate=pl.CostEstimate(flops=flops, bytes_accessed=moved, transcendentals=0),
    )(*args)


def unit(tokens):
    width = tokens.shape[1]
    centered = tokens - jnp.sum(tokens, axis=1, keepdims=True) / width
    inv_scale = lax.rsqrt(jnp.sum(centered * centered, axis=1, keepdims=True) / width + epsilon)
    return centered * inv_scale, inv_scale


def pack_body(tokens, cotangent, w_in, w_out, out, block):
    hidden = w_in.shape[1]
    block[0] = w_in[...]
    block[1, :hidden] = w_out[:, :hidden]
    block[1, hidden:] = w_out[:, hidden:]
    features = out.shape[2]
    normed = unit(tokens[...].astype(f32))[0]
    grads = cotangent[...].astype(f32)
    for part in range(ZH):
        cut = slice(part * features, (part + 1) * features)
        pair = jnp.concatenate([normed[:, cut], grads[:, cut]], axis=0).astype(bf16)
        out[part * ZL : (part + 1) * ZL] = jnp.broadcast_to(pair[None], (ZL,) + pair.shape)


def place(here, step, width):
    return pl.multiple_of(lax.rem(here + step, Y) * width, 128)


def line_up(rows, other, index, cut):
    return jnp.concatenate([ref[at, index, :, cut] for ref in (rows, other) for at in range(X)], axis=0)


def hidden_body(here, rows, other, b0, b1, b3, far_in, far_out, out):
    width, hidden = far_in.shape
    pre = grad = None
    for step, (ins, cols) in enumerate(
        ((b0.at[0], b0.at[1]), (b1.at[0], b1.at[1]), (far_in, far_out), (b3.at[0], b3.at[1]))
    ):
        at = place(here[0], step, width)
        left = line_up(rows, other, 0, pl.ds(at, width))
        terms = [dot(left, ins[...])]
        for part in range(width // hidden):
            cut = pl.ds(pl.multiple_of(at + part * hidden, 128), hidden)
            right = line_up(rows, other, 1, cut)
            terms.append(dot(right, cols[part * hidden : (part + 1) * hidden], LAST))
        one, two = terms[0], sum(terms[1:])
        pre = one if pre is None else pre + one
        grad = two if grad is None else grad + two
    out[0] = pre.astype(bf16)
    out[1] = grad.astype(bf16)


def split_body(rows, out):
    width = out.shape[3]
    for step in range(Y):
        for index in range(2):
            cut = slice(step * width, (step + 1) * width)
            out[step, index] = jnp.concatenate([rows[at, index, :, cut] for at in range(X)], axis=0)


def output_body(here, parts, b0, b1, b3, far_in, far_out, pair, keep, give):
    width, hidden = far_in.shape
    half = keep.shape[1]
    value = parts[0, 0].astype(f32) + parts[1, 0].astype(f32)
    upstream = parts[0, 1].astype(f32) + parts[1, 1].astype(f32)
    square = value * value
    curve = jnp.tanh(RATE * (value + CUBE * (square * value)))
    chance = 0.5 * (1.0 + curve)
    slope = chance + 0.5 * value * (1.0 - curve * curve) * (RATE * (1.0 + 3.0 * CUBE * square))
    act = (value * chance).astype(bf16)
    pre_grad = (upstream * slope).astype(bf16)
    pair[0] = act
    pair[1] = pre_grad
    for step, (ins, cols) in enumerate(
        ((b0.at[0], b0.at[1]), (b1.at[0], b1.at[1]), (far_in, far_out), (b3.at[0], b3.at[1]))
    ):
        at = place(here[0], step, width)
        term = dot(pre_grad, ins[...], LAST)
        keep[1, :, pl.ds(at, width)] = term[:half]
        give[1, :, pl.ds(at, width)] = term[half:].astype(bf16)
        for part in range(width // hidden):
            cut = pl.ds(pl.multiple_of(at + part * hidden, 128), hidden)
            term = dot(act, cols[part * hidden : (part + 1) * hidden])
            keep[0, :, cut] = term[:half]
            give[0, :, cut] = term[half:].astype(bf16)


def weight_body(here, p0, p1, p2, p3, mine, first, second, grad_w_in, grad_w_out):
    def every(index):
        found = []
        for step in range(Y):
            at = lax.rem(here[0] + Y - step, Y)
            low = first[lax.rem(at, Y // 2), index]
            high = second[lax.rem(at, Y // 2), index]
            found += [mine[at, index], jnp.where(at < Y // 2, low, high)]
        return jnp.concatenate(found, axis=0)

    full = [jnp.concatenate([ref[index] for ref in (p0, p1, p2, p3)], axis=0) for index in range(2)]
    grad_w_in[...] = dot(every(0), full[1], FIRST)
    grad_w_out[...] = dot(full[0], every(1), FIRST)


def add_body(keep, far, out):
    rows = out.shape[2]
    for step in range(X):
        at = slice(step * rows, (step + 1) * rows)
        out[step] = (keep[:, at] + far[:, at].astype(f32)).astype(bf16)


def sum_body(parts, out):
    first, second = (
        sum(parts[step, index].astype(f32) for step in range(X)).astype(bf16).astype(f32) for index in range(2)
    )
    for row in range(out.shape[0]):
        cut = slice(row, row + 1)
        out[row] = jnp.concatenate([first[cut], second[cut]], axis=0).astype(bf16)


def final_body(tokens, cotangent, sums, mixed, grad_tokens):
    features = sums.shape[2]
    tokens_wide = tokens[...].astype(f32)
    unit_rows, inv_scale = unit(tokens_wide)
    halves = [
        jnp.sum(sums[part * ZL : (part + 1) * ZL].astype(f32), axis=0) for part in range(ZH)
    ]
    whole = jnp.concatenate(halves, axis=1)
    count = ZH * features
    mixed[...] = (tokens_wide + whole[0:1]).astype(bf16)
    normed_grad = whole[1:2]
    inner = jnp.sum(normed_grad * unit_rows, axis=1, keepdims=True) / count
    mean = jnp.sum(normed_grad, axis=1, keepdims=True) / count
    through = inv_scale * (normed_grad - mean - unit_rows * inner)
    grad_tokens[...] = (cotangent[...].astype(f32) + through).astype(bf16)


def local(tokens, w_in, w_out, cotangent):
    width, hidden = w_in.shape
    features = Y * width
    count = X * ZL * ZH * CORE
    half = count // CORE
    here = lax.axis_index("y").reshape(1).astype(jnp.int32)
    shape = jax.ShapeDtypeStruct
    work = 4 * count * features * hidden

    both, block = call(
        pack_body,
        [shape((ZH * ZL, 2, features), bf16), shape((2, width, hidden), bf16)],
        tokens, cotangent, w_in, w_out,
    )
    both, block = lax.optimization_barrier((both, block))
    below, above = shift(block, "y", 1), shift(block, "y", -1)
    both = trade(both, FAR).transpose(1, 0, 2)
    rows = trade(jnp.broadcast_to(both, (X,) + both.shape), "x")
    far_in, far_out = shift(below[0], "y", 1), shift(above[1], "y", -1)
    (mine,) = call(split_body, [shape((Y, 2, half, width), bf16)], rows)
    other = swap(rows, "core")
    far_in, far_out, mine = lax.optimization_barrier((far_in, far_out, mine))
    mine = trade(mine, "y")
    blocks = (block, above, below, far_in, far_out)

    (parts,) = call(hidden_body, [shape((2, count, hidden), bf16)], here, rows, other, *blocks, flops=work)
    parts, mine = lax.optimization_barrier((lax.all_gather(parts, "zh"), mine))
    pair, keep, give = call(
        output_body,
        [shape((2, count, hidden), bf16), shape((2, half, features), f32), shape((2, half, features), bf16)],
        here, parts, *blocks, flops=work,
    )

    (sums,) = call(add_body, [shape((X, 2, half // X, features), bf16)], keep, swap(give, "core"))
    sums, pair = lax.optimization_barrier((sums, pair))
    side = (shift(pair, "y", 1), shift(pair, "y", 3))
    sums, side = lax.optimization_barrier((trade(sums, "x"), side))
    (sums,) = call(sum_body, [shape((half // X, 2, features), bf16)], sums)
    sums, mine, last = lax.optimization_barrier((sums, mine, pair))
    sums = trade(sums, FAR)
    held = (pair, side[0], shift(last, "y", 2), side[1])
    theirs = [swap(piece, "core") for piece in (mine[: Y // 2], mine[Y // 2 :])]

    grad_w_in, grad_w_out = call(
        weight_body,
        [shape((width, hidden), f32), shape((hidden, width), f32)],
        here, *held, mine, *theirs, flops=work,
    )

    sums, grad_w_in, grad_w_out = lax.optimization_barrier((sums, grad_w_in, grad_w_out))
    mixed, grad_tokens = call(
        final_body, [shape(tokens.shape, bf16)] * 2, tokens, cotangent, sums
    )
    return (mixed, grad_tokens, grad_w_in, grad_w_out)


def solution(mesh):
    fine = Mesh(mesh.devices.reshape(SIZES), AXES)
    dp, mp = ("zh", "y"), ("zl", "x", "core")
    return jax.shard_map(
        local,
        mesh=fine,
        in_specs=(P(dp + mp, None), P(dp, mp), P(mp, dp), P(dp + mp, None)),
        out_specs=(P(dp + mp, None), P(dp + mp, None), P(dp, mp), P(mp, dp)),
        check_vma=False,
    )
```
